128 devices in a mesh: seq: 32 (over x, z, y_lo), head: 4 (over y_hi, core).
Axes of the slice: x: 4, y: 4 (y_hi: 2, y_lo: 2; y = y_hi * 2 + y_lo), z: 4, core: 2. Of those that a mesh axis runs over, the one named last changes fastest.
Arguments:
- query: bfloat16 [65536, 1024], P('seq', 'head'), may hold values from -9 to 9
- key: bfloat16 [65536, 1024], P('seq', 'head'), may hold values from -9 to 9
- value: bfloat16 [65536, 1024], P('seq', 'head'), may hold values from -6 to 6
- offsets: int32 [5, 16], P(None, 'head'), may hold values from 0 to 63, as said below
Outputs:
- attended: bfloat16 [65536, 1024], P('seq', 'head')
The draws below stay inside these ranges and needn't reach their ends.
Inputs may be any that keep to these rules, and one draw needn't show every extreme that they name: offsets[0, h] is 0; offsets[l, h] lies below the rate of level l: 1, 4, 4, 16, 64; at every level some head takes the largest value.
All inputs are finite; a program needn't handle non-finite values.
Results may differ from the reference program's by a relative error of at most 0.0046.
Values may be sent and summed in bfloat16 or wider, within the bound.
No kernel may reach another device: no remote copies, remote signals or barrier semaphores. Data moves between devices by JAX's collectives and lax.ppermute only.
A program may use at most 320 MiB of HBM per device.

```python
import jax
import jax.numpy as jnp
from jax import lax

H = 16
LEVELS = 5
SEG = 512
TOK_DEV = 2048
D = 1024
TOKENS = 65536
RATE1 = 4
RATE2 = 4
RATE3 = 16
RATE4 = 64


def entries(key, salt):
    noise = jax.random.normal(jax.random.fold_in(key, salt), (TOKENS, D), jnp.float32)
    return jnp.clip(noise, -6.0, 6.0)


def draw_query(key, part):
    return entries(key, 1).astype(jnp.bfloat16)


def draw_key(key, part):
    return entries(key, 2).astype(jnp.bfloat16)


def draw_offsets(key, part):
    rates = jnp.array([1, RATE1, RATE2, RATE3, RATE4], jnp.int32)
    drawn = jax.random.randint(key, (LEVELS, H), 0, rates[:, None]).astype(jnp.int32)
    chosen = jax.random.randint(jax.random.fold_in(key, 3), (LEVELS,), 0, H).astype(jnp.int32)
    hit = jnp.arange(H, dtype=jnp.int32)[None, :] == chosen[:, None]
    return jnp.where(hit, rates[:, None] - 1, drawn).astype(jnp.int32)


def level_of(rng, shape, cuts, least, largest):
    factor_of, own = 1.0, jax.random.fold_in(rng, 6)
    for dim, parts in cuts:
        draws = jnp.exp(jax.random.uniform(jax.random.fold_in(own, dim), (parts,), jnp.float32, least / len(cuts), largest / len(cuts)))
        factor_of = factor_of * jnp.repeat(draws, shape[dim] // parts).reshape([-1 if axis == dim else 1 for axis in range(len(shape))])
    return factor_of


def bell_draw(own_key, shape, scale, limit, split=(), kind=jnp.bfloat16):
    level = level_of(own_key, shape, split, -0.22, 0.18) if split else 1.0
    entries = jax.random.normal(own_key, shape, jnp.float32) * scale * level
    return jnp.minimum(jnp.maximum(entries, -limit), limit).astype(kind)


def setup_inputs(seed: int = 0) -> dict:
    splits = jax.random.split(jax.random.key(seed), 5)
    query = draw_query(jax.random.fold_in(splits[4], 71), 0)
    key = draw_key(jax.random.fold_in(splits[4], 71), 0)
    value = bell_draw(splits[2], (TOKENS, D), 1.0, 6.0, ((0, 32), (1, 4)))
    offsets = draw_offsets(jax.random.fold_in(splits[4], 71), 0)
    return dict(query=query, key=key, value=value, offsets=offsets)


NEG = -1e30


def pick_rows(x, rate, offs):
    rows, width = x.shape
    heads = offs.shape[0]
    shaped = x.reshape(rows // rate, rate, heads, width // heads)
    index = offs.astype(jnp.int32)[None, None, :, None]
    return jnp.take_along_axis(shaped, index, axis=1)[:, 0]


def attend(query_rows, key_rows, value_rows):
    score_scale = query_rows.shape[-1] ** -0.5
    logit_scores = jnp.einsum("auc,euc->uae", query_rows.astype(jnp.float32), key_rows.astype(jnp.float32)) * score_scale
    top = jnp.max(logit_scores, axis=2, keepdims=True)
    attention_probs = jnp.exp(logit_scores - top)
    total = jnp.sum(attention_probs, axis=2)
    rounded_probs = attention_probs.astype(jnp.bfloat16).astype(jnp.float32)
    mixed_values = jnp.einsum("xjy,yxz->jxz", rounded_probs, value_rows.astype(jnp.float32))
    return mixed_values / total.T[:, :, None], (top[:, :, 0] + jnp.log(total)).T


def spread(out, lse, rate, offs):
    count, heads, size = out.shape
    hit = jnp.arange(rate)[:, None] == offs[None, :]
    full_out = jnp.where(hit[None, :, :, None], out[:, None], 0.0).reshape(count * rate, heads, size)
    full_lse = jnp.where(hit[None], lse[:, None], NEG).reshape(count * rate, heads)
    return full_out, full_lse


def level(query, key, value, offs, span, rate):
    query_rows = pick_rows(query, rate, offs)
    key_rows = pick_rows(key, rate, offs)
    value_rows = pick_rows(value, rate, offs)
    count = span // rate
    groups = query_rows.shape[0] // count

    def one(index):
        def take(a):
            return lax.dynamic_slice_in_dim(a, index * count, count, 0)
        return attend(take(query_rows), take(key_rows), take(value_rows))

    out, lse = lax.map(one, jnp.arange(groups).astype(jnp.int32))
    out = out.reshape(groups * count, out.shape[2], out.shape[3])
    lse = lse.reshape(groups * count, lse.shape[2])
    return spread(out, lse, rate, offs)


def blend(state, found):
    top, weight, acc = state
    out, lse = found
    new = jnp.maximum(top, lse)
    keep = jnp.exp(top - new)
    fresh = jnp.exp(lse - new)
    return new, weight * keep + fresh, acc * keep[:, :, None] + fresh[:, :, None] * out


def reference(query, key, value, offsets):
    spans = (SEG, TOK_DEV, 4 * TOK_DEV, TOKENS // 2, TOKENS)
    rates = (1, RATE1, RATE2, RATE3, RATE4)
    out0, lse0 = level(query, key, value, offsets[0], spans[0], rates[0])
    state = (lse0, jnp.ones(lse0.shape, jnp.float32), out0)
    for index in range(1, LEVELS):
        state = blend(state, level(query, key, value, offsets[index], spans[index], rates[index]))
    top, weight, acc = state
    return (acc / weight[:, :, None]).reshape(TOKENS, D).astype(jnp.bfloat16)
```

```python
import jax
import jax.numpy as jnp
from jax import lax
from jax.experimental import pallas as pl
from jax.experimental.pallas import tpu as pltpu
from jax.sharding import PartitionSpec as P

SEG = 512
RATE1 = 4
bf16 = jnp.bfloat16
f32 = jnp.float32
LANES = 128
HALF = 64
VMEM = pltpu.VMEM


def dot_nt(a, b):
    return lax.dot_general(a, b, (((1,), (1,)), ((), ())), preferred_element_type=f32)


def dot_nn(a, b):
    return lax.dot_general(a, b, (((1,), (0,)), ((), ())), preferred_element_type=f32)


def half_mask(rows, half):
    lane = lax.broadcasted_iota(jnp.int32, (rows, LANES), 1)
    return lax.div(lane, HALF) == half


def swap_halves(x):
    return pltpu.roll(x, HALF, 1)


def softmax_tile(q, keys, values, vl):
    scores = [dot_nt(q, k) for k in keys]
    top = scores[0].max(axis=1, keepdims=True)
    for s in scores[1:]:
        top = jnp.maximum(top, s.max(axis=1, keepdims=True))
    acc = None
    for s, v in zip(scores, values):
        part = dot_nn(jnp.exp(s - top).astype(bf16), v)
        acc = part if acc is None else acc + part
    return jnp.where(vl, acc / swap_halves(acc), top + jnp.log(acc))


def merge(vl, one, lse_one, two, lse_two):
    gap = lse_two - lse_one
    small = jnp.exp(-jnp.abs(gap))
    ahead = gap > 0.0
    big_out = jnp.where(ahead, two, one)
    small_out = jnp.where(ahead, one, two)
    weight = 1.0 + small
    out = (big_out + small * small_out) / weight
    return jnp.where(vl, out, jnp.maximum(lse_one, lse_two) + jnp.log(weight))


def spread_lse(tile, vl):
    return jnp.where(vl, swap_halves(tile), tile)


def encode(tile, vl, half):
    lane = lax.broadcasted_iota(jnp.int32, tile.shape, 1)
    spot = lax.rem(lane, HALF)
    first = tile.astype(bf16).astype(f32)
    rest = tile - first
    second = rest.astype(bf16).astype(f32)
    third = rest - second
    coded = jnp.where(spot == 0, first, jnp.where(spot == 1, second, third))
    return jnp.where(vl, tile, coded).astype(bf16)


def decode_lse(coded, half):
    row = lax.broadcasted_iota(jnp.int32, (LANES, LANES), 0)
    pick = jnp.logical_and(lax.div(row, HALF) != half, lax.rem(row, HALF) < 3)
    return dot_nn(coded, jnp.where(pick, 1.0, 0.0).astype(bf16))


def widen(src, dst):
    rows = src.shape[0]
    step = min(rows, 512)

    @pl.loop(0, rows // step)
    def _(i):
        part = pl.ds(pl.multiple_of(i * step, step), step)
        for p in range(src.shape[1] // LANES):
            dst[p, part, :] = src[part, p * LANES : (p + 1) * LANES].astype(f32)


def pack_kernel(levels, offs, q_ref, k_ref, v_ref, *rest):
    near_out, far_out, (qs, ks, vs) = rest[0:4], rest[4:8], rest[8:11]
    mine = lax.rem(lax.axis_index("seq"), 4)
    widen(q_ref, qs)
    widen(k_ref, ks)
    widen(v_ref, vs)
    for d in range(4):
        head = mine ^ d
        pair, half = lax.div(head, 2), lax.rem(head, 2)
        base = [0, 0]
        for what in ("kv", "q"):
            for index, (level, count, rate, near) in enumerate(levels):
                off = offs[level, head]
                ref = near_out[d] if near else far_out[d]
                at = base[near]
                if what == "kv":
                    vl = half_mask(count, half)
                    k = ks[pair, pl.ds(off, count, rate), :]
                    v = vs[pair, pl.ds(off, count, rate), :]
                    ref[at : at + count, :] = jnp.where(vl, v, swap_halves(k)).astype(bf16)
                    base[near] = at + count
                else:
                    few = count // 2
                    vl = half_mask(few, half)
                    q_one = qs[pair, pl.ds(off, few, rate), :]
                    q_two = qs[pair, pl.ds(off + few * rate, few, rate), :]
                    tile = jnp.where(vl, q_two, swap_halves(q_one))
                    ref[at : at + few, :] = (tile * 0.125).astype(bf16)
                    base[near] = at + few


def local_kernel(rate, offs, q_ref, k_ref, v_ref, t_ref, qs, ks, vs):
    rows = q_ref.shape[0]
    count = rows // rate
    zero, one = jnp.asarray(0, bf16), jnp.asarray(1, bf16)
    scale = jnp.asarray(0.125, bf16)

    @pl.loop(0, rows // SEG)
    def _(s):
        part = pl.ds(pl.multiple_of(s * SEG, SEG), SEG)
        for h in range(4):
            cols = slice(h // 2 * LANES, (h // 2 + 1) * LANES)
            vl = half_mask(SEG, h % 2)
            q = q_ref[part, cols] * scale
            k = jnp.where(vl, k_ref[part, cols], zero)
            v = jnp.where(vl, v_ref[part, cols], one)
            t_ref[h, part, :] = softmax_tile(q, [k], [v], vl)

    widen(q_ref, qs)
    widen(k_ref, ks)
    widen(v_ref, vs)
    for h in range(4):
        off = offs[1, h]
        vl = half_mask(count, h % 2)
        picked = pl.ds(off, count, rate)
        q = (qs[h // 2, picked, :] * 0.125).astype(bf16)
        k = jnp.where(vl, ks[h // 2, picked, :], 0.0).astype(bf16)
        v = jnp.where(vl, vs[h // 2, picked, :], 1.0).astype(bf16)
        new = softmax_tile(q, [k], [v], vl)
        old = t_ref[h, picked, :]
        t_ref[h, picked, :] = merge(vl, old, spread_lse(old, vl), new, spread_lse(new, vl))


def keys_values(tile, half):
    vl = half_mask(tile.shape[0], half)
    zero, one = jnp.asarray(0, bf16), jnp.asarray(1, bf16)
    return jnp.where(vl, zero, tile), jnp.where(vl, tile, one)


def near_kernel(count, *refs):
    ins, outs = refs[:4], refs[4:]
    half = lax.rem(lax.axis_index("seq"), 2)
    keys, values = zip(*[keys_values(r[:count, :], half) for r in ins])
    few = count // 2
    vl = half_mask(few, half)
    for d in range(4):
        tile = ins[d][count : count + few, :]
        for part in range(2):
            q = tile if part == 0 else swap_halves(tile.astype(f32)).astype(bf16)
            found = softmax_tile(q, keys, values, vl)
            outs[d][part * few : (part + 1) * few, :] = encode(found, vl, half)


def far_kernel(mid, top, *refs):
    far, gathered, outs = refs[:4], refs[4:8], refs[8:12]
    half = lax.rem(lax.axis_index("seq"), 2)
    base = mid + top
    blocks = (
        (0, 4 * mid, base, mid // 2, 0),
        (4 * mid, gathered[0].shape[0] - 4 * mid, base + mid // 2, top // 2, mid),
    )
    for key_at, key_count, q_at, few, out_at in blocks:
        keys, values = zip(
            *[keys_values(r[key_at : key_at + key_count, :], half) for r in gathered]
        )
        tile = jnp.concatenate([r[q_at : q_at + few, :].astype(f32) for r in far], axis=0)
        vl = half_mask(4 * few, half)
        for part in range(2):
            q = (tile if part == 0 else swap_halves(tile)).astype(bf16)
            found = encode(softmax_tile(q, keys, values, vl), vl, half).astype(f32)
            for d in range(4):
                at = out_at + part * few
                outs[d][at : at + few, :] = found[d * few : (d + 1) * few, :].astype(bf16)


def final_kernel(levels, offs, t_ref, *refs):
    near, far, out_ref, ts = refs[:4], refs[4:8], refs[8], refs[9]
    mine = lax.rem(lax.axis_index("seq"), 4)
    rows = out_ref.shape[0]
    ts[...] = t_ref[...]
    for d in range(4):
        head = mine ^ d
        half = lax.rem(head, 2)
        at = 0
        for level, count, rate, is_near in levels:
            off = offs[level, head]
            if is_near:
                coded = near[d][...]
            else:
                coded = far[d][at : at + count, :]
                at += count
            vl = half_mask(count, half)
            picked = pl.ds(off, count, rate)
            old = ts[head, picked, :]
            ts[head, picked, :] = merge(
                vl, old, spread_lse(old, vl), coded.astype(f32), decode_lse(coded, half)
            )
    vl = half_mask(rows, 0)
    for p in range(2):
        out_ref[:, p * LANES : (p + 1) * LANES] = jnp.where(
            vl, ts[2 * p, :, :], ts[2 * p + 1, :, :]
        ).astype(bf16)


def call(body, name, outs, n_in, scratch=(), smem=True, flops=0, bytes_moved=0, exps=0):
    whole = pl.BlockSpec(memory_space=VMEM)
    first = [pl.BlockSpec(memory_space=pltpu.SMEM)] if smem else []
    return pl.pallas_call(
        body,
        name=name,
        out_shape=outs,
        in_specs=first + [whole] * n_in,
        out_specs=jax.tree.map(lambda _: whole, outs),
        scratch_shapes=list(scratch),
        compiler_params=pltpu.CompilerParams(vmem_limit_bytes=56 << 20),
        cost_estimate=pl.CostEstimate(flops=flops, bytes_accessed=bytes_moved, transcendentals=exps),
    )


def swapped(shard, bits):
    return lax.ppermute(shard, "seq", [(i, i ^ bits) for i in range(lax.axis_size("seq"))])


def per_device(query, key, value, offsets):
    rows, width = query.shape
    places = lax.axis_size("seq")
    rate_three = RATE1 * places // 8
    rate_four = 4 * rate_three
    near_count, mid, top = rows // RATE1, rows // rate_three, rows // rate_four
    levels = (
        (2, near_count, RATE1, True),
        (3, mid, rate_three, False),
        (4, top, rate_four, False),
    )
    near_rows = near_count * 3 // 2
    far_rows = (mid + top) * 3 // 2
    wide = VMEM((2, rows, LANES), f32)

    def tile(n, kind=bf16):
        return jax.ShapeDtypeStruct((n, LANES), kind)

    def packed(*args):
        return call(
            lambda *refs: pack_kernel(levels, *refs),
            "pack",
            [tile(near_rows)] * 4 + [tile(far_rows)] * 4,
            3,
            (wide, wide, wide),
            bytes_moved=5 << 20,
        )(*args)

    parts = packed(offsets, query, key, value)
    near_sent, far_sent = parts[:4], parts[4:]
    far_held = [far_sent[0]] + [swapped(far_sent[d], d) for d in (1, 2, 3)]
    near_held = [near_sent[0]] + [swapped(near_sent[d], d) for d in (1, 2, 3)]

    state = call(
        lambda *refs: local_kernel(RATE1, *refs),
        "local",
        jax.ShapeDtypeStruct((4, rows, LANES), f32),
        3,
        (wide, wide, wide),
        flops=6 << 30,
        bytes_moved=7 << 20,
        exps=5 << 20,
    )(offsets, query, key, value)

    own_mid = jnp.concatenate([r[:mid] for r in far_held], axis=0)
    own_top = jnp.concatenate([r[mid : mid + top] for r in far_held], axis=0)
    other_top = swapped(own_top, 16)
    held = jnp.concatenate([own_mid, own_top, other_top], axis=0)
    gathered = [held] + [swapped(held, b) for b in (4, 8, 12)]

    near_found = call(
        lambda *refs: near_kernel(near_count, *refs),
        "near",
        [tile(near_count)] * 4,
        4,
        smem=False,
        flops=6 << 30,
        bytes_moved=2 << 20,
        exps=4 << 20,
    )(*near_held)
    near_back = [near_found[0]] + [swapped(near_found[d], d) for d in (1, 2, 3)]

    far_found = call(
        lambda *refs: far_kernel(mid, top, *refs),
        "far",
        [tile(mid + top)] * 4,
        8,
        smem=False,
        flops=2 << 30,
        bytes_moved=2 << 20,
        exps=1 << 20,
    )(*far_held, *gathered)
    far_back = [far_found[0]] + [swapped(far_found[d], d) for d in (1, 2, 3)]

    return call(
        lambda *refs: final_kernel(levels, *refs),
        "final",
        jax.ShapeDtypeStruct((rows, width), bf16),
        9,
        (VMEM((4, rows, LANES), f32),),
        bytes_moved=6 << 20,
    )(offsets, state, *near_back, *far_back)


def solution(mesh):
    return jax.shard_map(
        per_device,
        mesh=mesh,
        in_specs=(P("seq", "head"), P("seq", "head"), P("seq", "head"), P(None, "head")),
        out_specs=P("seq", "head"),
        check_vma=False,
    )
```

```python
import jax
import jax.numpy as jnp
from jax import lax
from jax.experimental import pallas as pl
from jax.experimental.pallas import tpu as pltpu
from jax.sharding import PartitionSpec as P


SEG = 512
RATE1 = 4
bf16 = jnp.bfloat16
f32 = jnp.float32
LANES = 128
HALF = 64
VMEM = pltpu.VMEM


def dot_nt(a, b):
    return lax.dot_general(a, b, (((1,), (1,)), ((), ())), preferred_element_type=f32)


def dot_nn(a, b):
    return lax.dot_general(a, b, (((1,), (0,)), ((), ())), preferred_element_type=f32)


def half_mask(rows, half):
    lane = lax.broadcasted_iota(jnp.int32, (rows, LANES), 1)
    return lax.div(lane, HALF) == half


def swap_halves(x):
    return pltpu.roll(x, HALF, 1)


def softmax_tile(q, keys, values, vl):
    scores = [dot_nt(q, k) for k in keys]
    top = scores[0].max(axis=1, keepdims=True)
    for s in scores[1:]:
        top = jnp.maximum(top, s.max(axis=1, keepdims=True))
    acc = None
    for s, v in zip(scores, values):
        part = dot_nn(jnp.exp(s - top).astype(bf16), v)
        acc = part if acc is None else acc + part
    return jnp.where(vl, acc / swap_halves(acc), top + jnp.log(acc))


def merge(vl, one, lse_one, two, lse_two):
    gap = lse_two - lse_one
    small = jnp.exp(-jnp.abs(gap))
    ahead = gap > 0.0
    big_out = jnp.where(ahead, two, one)
    small_out = jnp.where(ahead, one, two)
    weight = 1.0 + small
    out = (big_out + small * small_out) / weight
    return jnp.where(vl, out, jnp.maximum(lse_one, lse_two) + jnp.log(weight))


def spread_lse(tile, vl):
    return jnp.where(vl, swap_halves(tile), tile)


def encode(tile, vl):
    lane = lax.broadcasted_iota(jnp.int32, tile.shape, 1)
    spot = lax.rem(lane, HALF)
    first = tile.astype(bf16).astype(f32)
    rest = tile - first
    second = rest.astype(bf16).astype(f32)
    third = rest - second
    coded = jnp.where(spot == 0, first, jnp.where(spot == 1, second, third))
    return jnp.where(vl, tile, coded).astype(bf16)


def decode_lse(coded, half):
    row = lax.broadcasted_iota(jnp.int32, (LANES, LANES), 0)
    pick = jnp.logical_and(lax.div(row, HALF) != half, lax.rem(row, HALF) < 3)
    return dot_nn(coded, jnp.where(pick, 1.0, 0.0).astype(bf16))


def widen(src, dst):
    rows = src.shape[0]
    step = min(rows, 512)

    @pl.loop(0, rows // step)
    def _(i):
        part = pl.ds(pl.multiple_of(i * step, step), step)
        for p in range(src.shape[1] // LANES):
            dst[p, part, :] = src[part, p * LANES : (p + 1) * LANES].astype(f32)


def fetch(offs_any, offs, sem):
    copy = pltpu.make_async_copy(offs_any, offs, sem)
    copy.start()
    return copy


def pack_kernel(levels, offs_any, q_any, k_any, v_any, *rest):
    near_out, far_out, (qs, ks, vs, qb, kb, vb, offs, sems) = rest[0:4], rest[4:8], rest[8:]
    mine = lax.rem(lax.axis_index("seq"), 4)
    copies = [fetch(k_any, kb, sems.at[0]), fetch(v_any, vb, sems.at[1])]
    copies += [fetch(q_any, qb, sems.at[2]), fetch(offs_any, offs, sems.at[3])]
    for copy, narrow, wide in zip(copies, (kb, vb, qb), (ks, vs, qs)):
        copy.wait()
        widen(narrow, wide)
    copies[3].wait()
    for d in range(4):
        head = mine ^ d
        pair, half = lax.div(head, 2), lax.rem(head, 2)
        base = [0, 0]
        for what in ("kv", "q"):
            for level, count, rate, near in levels:
                off = offs[level, head]
                ref = near_out[d] if near else far_out[d]
                at = base[near]
                if what == "kv":
                    vl = half_mask(count, half)
                    k = ks[pair, pl.ds(off, count, rate), :]
                    v = vs[pair, pl.ds(off, count, rate), :]
                    ref[at : at + count, :] = jnp.where(vl, v, swap_halves(k)).astype(bf16)
                    base[near] = at + count
                else:
                    few = count // 2
                    vl = half_mask(few, half)
                    q_one = qs[pair, pl.ds(off, few, rate), :]
                    q_two = qs[pair, pl.ds(off + few * rate, few, rate), :]
                    tile = jnp.where(vl, q_two, swap_halves(q_one))
                    ref[at : at + few, :] = (tile * 0.125).astype(bf16)
                    base[near] = at + few


def first_kernel(q_ref, k_ref, v_ref, t_ref):
    zero, one = jnp.asarray(0, bf16), jnp.asarray(1, bf16)
    scale = jnp.asarray(0.125, bf16)

    @pl.loop(0, q_ref.shape[0] // SEG)
    def _(s):
        part = pl.ds(pl.multiple_of(s * SEG, SEG), SEG)
        for h in range(4):
            cols = slice(h // 2 * LANES, (h // 2 + 1) * LANES)
            vl = half_mask(SEG, h % 2)
            q = q_ref[part, cols] * scale
            k = jnp.where(vl, k_ref[part, cols], zero)
            v = jnp.where(vl, v_ref[part, cols], one)
            t_ref[h, part, :] = softmax_tile(q, [k], [v], vl)


def second_kernel(rate, offs_any, q_ref, k_ref, v_ref, found_ref, qs, ks, vs, offs, sem):
    copy = fetch(offs_any, offs, sem)
    count = q_ref.shape[0] // rate
    widen(q_ref, qs)
    widen(k_ref, ks)
    widen(v_ref, vs)
    copy.wait()
    for h in range(4):
        vl = half_mask(count, h % 2)
        picked = pl.ds(offs[1, h], count, rate)
        q = (qs[h // 2, picked, :] * 0.125).astype(bf16)
        k = jnp.where(vl, ks[h // 2, picked, :], 0.0).astype(bf16)
        v = jnp.where(vl, vs[h // 2, picked, :], 1.0).astype(bf16)
        found_ref[h, :, :] = softmax_tile(q, [k], [v], vl)


def keys_values(tile, half):
    vl = half_mask(tile.shape[0], half)
    zero, one = jnp.asarray(0, bf16), jnp.asarray(1, bf16)
    return jnp.where(vl, zero, tile), jnp.where(vl, tile, one)


def near_kernel(count, *refs):
    ins, outs = refs[:4], refs[4:]
    half = lax.rem(lax.axis_index("seq"), 2)
    keys, values = zip(*[keys_values(r[:count, :], half) for r in ins])
    few = count // 2
    vl = half_mask(few, half)
    for d in range(4):
        tile = ins[d][count : count + few, :]
        for part in range(2):
            q = tile if part == 0 else swap_halves(tile.astype(f32)).astype(bf16)
            found = softmax_tile(q, keys, values, vl)
            outs[d][part * few : (part + 1) * few, :] = encode(found, vl)


def far_kernel(mid, top, *refs):
    far, gathered, tops, outs = refs[:4], refs[4:8], refs[8:12], refs[12:16]
    half = lax.rem(lax.axis_index("seq"), 2)
    base = mid + top
    blocks = (
        ([r[: 4 * mid, :] for r in gathered], base, mid // 2, 0),
        ([r[4 * mid :, :] for r in gathered] + [r[...] for r in tops], base + mid // 2, top // 2, mid),
    )
    for tiles, q_at, few, out_at in blocks:
        keys, values = zip(*[keys_values(t, half) for t in tiles])
        tile = jnp.concatenate([r[q_at : q_at + few, :].astype(f32) for r in far], axis=0)
        q = jnp.concatenate([tile, swap_halves(tile)], axis=0).astype(bf16)
        vl = half_mask(8 * few, half)
        found = encode(softmax_tile(q, keys, values, vl), vl).astype(f32)
        for part in range(2):
            for d in range(4):
                at, start = out_at + part * few, (part * 4 + d) * few
                outs[d][at : at + few, :] = found[start : start + few, :].astype(bf16)


def absorb(state, head, half, off, rate, coded):
    count = coded.shape[0]
    vl = half_mask(count, half)
    picked = pl.ds(off, count, rate)
    old = state[head, picked, :]
    state[head, picked, :] = merge(
        vl, old, spread_lse(old, vl), coded.astype(f32), decode_lse(coded, half)
    )


def blend_kernel(rate, offs_any, state_in, found_ref, *refs):
    near, state, offs, sem = refs[:4], refs[4], refs[5], refs[6]
    copy = fetch(offs_any, offs, sem)
    mine = lax.rem(lax.axis_index("seq"), 4)
    copy.wait()
    count = found_ref.shape[1]
    for h in range(4):
        vl = half_mask(count, h % 2)
        picked = pl.ds(offs[1, h], count, rate)
        old, new = state[h, picked, :], found_ref[h, :, :]
        state[h, picked, :] = merge(vl, old, spread_lse(old, vl), new, spread_lse(new, vl))
    for d in range(4):
        head = mine ^ d
        absorb(state, head, lax.rem(head, 2), offs[2, head], rate, near[d][...])


def final_kernel(levels, offs_any, state_in, *refs):
    far, state, out_ref, offs, sem = refs[:4], refs[4], refs[5], refs[6], refs[7]
    copy = fetch(offs_any, offs, sem)
    mine = lax.rem(lax.axis_index("seq"), 4)
    copy.wait()
    for d in range(4):
        head = mine ^ d
        at = 0
        for level, count, rate, near in levels:
            if not near:
                absorb(
                    state, head, lax.rem(head, 2), offs[level, head], rate, far[d][at : at + count, :]
                )
                at += count
    vl = half_mask(out_ref.shape[0], 0)
    for p in range(2):
        out_ref[:, p * LANES : (p + 1) * LANES] = jnp.where(
            vl, state[2 * p, :, :], state[2 * p + 1, :, :]
        ).astype(bf16)


def call(body, outs, spaces, scratch=(), flops=0, bytes_moved=0, exps=0, aliases=None):
    whole = pl.BlockSpec(memory_space=VMEM)
    place = {"v": whole, "a": pl.BlockSpec(memory_space=pltpu.HBM)}
    return pl.pallas_call(
        body,
        out_shape=outs,
        in_specs=[place[c] for c in spaces],
        out_specs=jax.tree.map(lambda _: whole, outs),
        scratch_shapes=list(scratch),
        input_output_aliases=aliases or {},
        compiler_params=pltpu.CompilerParams(vmem_limit_bytes=48 << 20),
        cost_estimate=pl.CostEstimate(flops=flops, bytes_accessed=bytes_moved, transcendentals=exps),
    )


def swapped(shard, bits):
    return lax.ppermute(
        shard, "seq", [(i, i ^ bits) for i in range(lax.axis_size("seq"))]
    )


def per_device(query, key, value, offsets):
    rows, width = query.shape
    places = lax.axis_size("seq")
    rate_three = RATE1 * places // 8
    rate_four = 4 * rate_three
    near_count, mid, top = rows // RATE1, rows // rate_three, rows // rate_four
    levels = (
        (2, near_count, RATE1, True),
        (3, mid, rate_three, False),
        (4, top, rate_four, False),
    )
    wide = VMEM((2, rows, LANES), f32)
    narrow = VMEM((rows, width), bf16)
    table = pltpu.SMEM(offsets.shape, jnp.int32)
    one_sem = pltpu.SemaphoreType.DMA

    def tile(n, kind=bf16):
        return jax.ShapeDtypeStruct((n, LANES), kind)

    state_shape = jax.ShapeDtypeStruct((4, rows, LANES), f32)
    parts = call(
        lambda *refs: pack_kernel(levels, *refs),
        [tile(near_count * 3 // 2)] * 4 + [tile((mid + top) * 3 // 2)] * 4,
        "aaaa",
        (wide, wide, wide, narrow, narrow, narrow, table, pltpu.SemaphoreType.DMA((4,))),
        bytes_moved=5 << 20,
    )(offsets, query, key, value)
    near_sent, far_sent = parts[:4], parts[4:]
    far_held = [far_sent[0]] + [swapped(far_sent[d], d) for d in (1, 2, 3)]
    near_held = [near_sent[0]] + [swapped(near_sent[d], d) for d in (1, 2, 3)]

    state = call(
        first_kernel, state_shape, "vvv", flops=4 << 30, bytes_moved=7 << 20, exps=4 << 20
    )(query, key, value)

    own_top = jnp.concatenate([r[mid : mid + top] for r in far_held], axis=0)
    held = jnp.concatenate([r[:mid] for r in far_held] + [own_top], axis=0)
    gathered = [held] + [swapped(held, b) for b in (12, 8, 4)]
    tops = [swapped(own_top, 16 + b) for b in (12, 8, 4, 0)]

    near_found = call(
        lambda *refs: near_kernel(near_count, *refs),
        [tile(near_count)] * 4,
        "vvvv",
        flops=6 << 30,
        bytes_moved=2 << 20,
        exps=4 << 20,
    )(*near_held)
    near_back = [near_found[0]] + [swapped(near_found[d], d) for d in (1, 2, 3)]

    found = call(
        lambda *refs: second_kernel(RATE1, *refs),
        jax.ShapeDtypeStruct((4, near_count, LANES), f32),
        "avvv",
        (wide, wide, wide, table, one_sem),
        flops=2 << 30,
        bytes_moved=4 << 20,
        exps=1 << 20,
    )(offsets, query, key, value)

    far_found = call(
        lambda *refs: far_kernel(mid, top, *refs),
        [tile(mid + top)] * 4,
        "v" * 12,
        flops=2 << 30,
        bytes_moved=2 << 20,
        exps=1 << 20,
    )(*far_held, *gathered, *tops)
    far_back = [far_found[0]] + [swapped(far_found[d], d) for d in (1, 2, 3)]

    state = call(
        lambda *refs: blend_kernel(RATE1, *refs),
        state_shape,
        "avvvvvv",
        (table, one_sem),
        bytes_moved=10 << 20,
        aliases={1: 0},
    )(offsets, state, found, *near_back)

    return call(
        lambda *refs: final_kernel(levels, *refs),
        [state_shape, jax.ShapeDtypeStruct((rows, width), bf16)],
        "avvvvv",
        (table, one_sem),
        bytes_moved=6 << 20,
        aliases={1: 0},
    )(offsets, state, *far_back)[1]


def solution(mesh):
    return jax.shard_map(
        per_device,
        mesh=mesh,
        in_specs=(P("seq", "head"), P("seq", "head"), P("seq", "head"), P(None, "head")),
        out_specs=P("seq", "head"),
        check_vma=False,
    )
```

```python
import jax
import jax.numpy as jnp
from jax import lax
from jax.experimental import pallas as pl
from jax.experimental.pallas import tpu as pltpu
from jax.sharding import PartitionSpec as P


SEG = 512
PACK_MIB = 24
RATE1 = 4
bf16 = jnp.bfloat16
f32 = jnp.float32
LANES = 128
HALF = 64
VMEM = pltpu.VMEM


def dot_nt(a, b):
    return lax.dot_general(a, b, (((1,), (1,)), ((), ())), preferred_element_type=f32)


def dot_nn(a, b):
    return lax.dot_general(a, b, (((1,), (0,)), ((), ())), preferred_element_type=f32)


def half_mask(rows, half):
    lane = lax.broadcasted_iota(jnp.int32, (rows, LANES), 1)
    return lax.div(lane, HALF) == half


def swap_halves(x):
    return pltpu.roll(x, HALF, 1)


def softmax_tile(q, keys, values, vl):
    scores = [dot_nt(q, k) for k in keys]
    top = scores[0].max(axis=1, keepdims=True)
    for s in scores[1:]:
        top = jnp.maximum(top, s.max(axis=1, keepdims=True))
    acc = None
    for s, v in zip(scores, values):
        part = dot_nn(jnp.exp(s - top).astype(bf16), v)
        acc = part if acc is None else acc + part
    return jnp.where(vl, acc / swap_halves(acc), top + jnp.log(acc))


def merge(vl, one, lse_one, two, lse_two):
    gap = lse_two - lse_one
    small = jnp.exp(-jnp.abs(gap))
    ahead = gap > 0.0
    big_out = jnp.where(ahead, two, one)
    small_out = jnp.where(ahead, one, two)
    weight = 1.0 + small
    out = (big_out + small * small_out) / weight
    return jnp.where(vl, out, jnp.maximum(lse_one, lse_two) + jnp.log(weight))


def spread_lse(tile, vl):
    return jnp.where(vl, swap_halves(tile), tile)


def encode(tile, vl):
    lane = lax.broadcasted_iota(jnp.int32, tile.shape, 1)
    spot = lax.rem(lane, HALF)
    first = tile.astype(bf16).astype(f32)
    rest = tile - first
    second = rest.astype(bf16).astype(f32)
    third = rest - second
    coded = jnp.where(spot == 0, first, jnp.where(spot == 1, second, third))
    return jnp.where(vl, tile, coded).astype(bf16)


def decode_lse(coded, half):
    row = lax.broadcasted_iota(jnp.int32, (LANES, LANES), 0)
    pick = jnp.logical_and(lax.div(row, HALF) != half, lax.rem(row, HALF) < 3)
    return dot_nn(coded, jnp.where(pick, 1.0, 0.0).astype(bf16))


def widen(src, dst):
    rows = src.shape[0]
    step = min(rows, 512)

    @pl.loop(0, rows // step)
    def _(i):
        part = pl.ds(pl.multiple_of(i * step, step), step)
        for p in range(src.shape[1] // LANES):
            dst[p, part, :] = src[part, p * LANES : (p + 1) * LANES].astype(f32)


def fetch(offs_any, offs, sem):
    copy = pltpu.make_async_copy(offs_any, offs, sem)
    copy.start()
    return copy


def pack_kernel(levels, offs_any, q_any, k_any, v_any, *rest):
    near_out, far_out, (qb, kb, vb, qs, ks, vs, offs, sems) = rest[0:4], rest[4:8], rest[8:]
    mine = lax.rem(lax.axis_index("seq"), 4)
    copies = [fetch(k_any, kb, sems.at[0]), fetch(v_any, vb, sems.at[1])]
    copies += [fetch(q_any, qb, sems.at[2]), fetch(offs_any, offs, sems.at[3])]
    for copy, narrow, wide in zip(copies, (kb, vb, qb), (ks, vs, qs)):
        copy.wait()
        widen(narrow, wide)
    copies[3].wait()
    for d in range(4):
        head = mine ^ d
        pair, half = lax.div(head, 2), lax.rem(head, 2)
        base = [0, 0]
        for what in ("kv", "q"):
            for level, count, rate, near in levels:
                off = offs[head, level]
                ref = near_out[d] if near else far_out[d]
                at = base[near]
                if what == "kv":
                    vl = half_mask(count, half)
                    k = ks[pair, pl.ds(off, count, rate), :]
                    v = vs[pair, pl.ds(off, count, rate), :]
                    ref[at : at + count, :] = jnp.where(vl, v, swap_halves(k)).astype(bf16)
                    base[near] = at + count
                else:
                    few = count // 2
                    vl = half_mask(few, half)
                    q_one = qs[pair, pl.ds(off, few, rate), :]
                    q_two = qs[pair, pl.ds(off + few * rate, few, rate), :]
                    tile = jnp.where(vl, q_two, swap_halves(q_one))
                    ref[at : at + few, :] = (tile * 0.125).astype(bf16)
                    base[near] = at + few


def first_kernel(pair, q_ref, k_ref, v_ref, *rest):
    t_ref = rest[-1]
    zero, one = jnp.asarray(0, bf16), jnp.asarray(1, bf16)
    scale = jnp.asarray(0.125, bf16)
    cols = slice(pair * LANES, (pair + 1) * LANES)

    @pl.loop(0, q_ref.shape[0] // SEG)
    def _(s):
        part = pl.ds(pl.multiple_of(s * SEG, SEG), SEG)
        for h in range(2):
            vl = half_mask(SEG, h)
            q = q_ref[part, cols] * scale
            k = jnp.where(vl, k_ref[part, cols], zero)
            v = jnp.where(vl, v_ref[part, cols], one)
            t_ref[h, part, :] = softmax_tile(q, [k], [v], vl)


def second_kernel(rate, offs_any, qs, ks, vs, found_ref, offs, sem):
    copy = fetch(offs_any, offs, sem)
    count = found_ref.shape[1]
    copy.wait()
    for h in range(4):
        vl = half_mask(count, h % 2)
        picked = pl.ds(offs[h, 1], count, rate)
        q = (qs[h // 2, picked, :] * 0.125).astype(bf16)
        k = jnp.where(vl, ks[h // 2, picked, :], 0.0).astype(bf16)
        v = jnp.where(vl, vs[h // 2, picked, :], 1.0).astype(bf16)
        found_ref[h, :, :] = softmax_tile(q, [k], [v], vl)


def keys_values(tile, half):
    vl = half_mask(tile.shape[0], half)
    zero, one = jnp.asarray(0, bf16), jnp.asarray(1, bf16)
    return jnp.where(vl, zero, tile), jnp.where(vl, tile, one)


def near_kernel(count, *refs):
    ins, outs = refs[:4], refs[4:]
    half = lax.rem(lax.axis_index("seq"), 2)
    keys, values = zip(*[keys_values(r[:count, :], half) for r in ins])
    few = count // 2
    vl = half_mask(few, half)
    for d in range(4):
        tile = ins[d][count : count + few, :]
        for part in range(2):
            q = tile if part == 0 else swap_halves(tile.astype(f32)).astype(bf16)
            found = softmax_tile(q, keys, values, vl)
            outs[d][part * few : (part + 1) * few, :] = encode(found, vl)


def far_kernel(mid, top, *refs):
    far, gathered, outs = refs[:4], refs[4:8], refs[8:12]
    half = lax.rem(lax.axis_index("seq"), 2)
    base = mid + top
    blocks = (
        ([r[: 4 * mid, :] for r in gathered], base, mid // 2, 0),
        ([r[4 * mid :, :] for r in gathered], base + mid // 2, top // 2, mid),
    )
    for tiles, q_at, few, out_at in blocks:
        keys, values = zip(*[keys_values(t, half) for t in tiles])
        tile = jnp.concatenate([r[q_at : q_at + few, :].astype(f32) for r in far], axis=0)
        q = jnp.concatenate([tile, swap_halves(tile)], axis=0).astype(bf16)
        vl = half_mask(8 * few, half)
        found = encode(softmax_tile(q, keys, values, vl), vl).astype(f32)
        for part in range(2):
            for d in range(4):
                at, start = out_at + part * few, (part * 4 + d) * few
                outs[d][at : at + few, :] = found[start : start + few, :].astype(bf16)


def absorb(state, head, off, rate, new, lse_new):
    count = new.shape[0]
    vl = half_mask(count, lax.rem(head, 2))
    picked = pl.ds(off, count, rate)
    old = state[head, picked, :]
    state[head, picked, :] = merge(vl, old, spread_lse(old, vl), new, lse_new)


def absorb_coded(state, head, off, rate, coded):
    absorb(state, head, off, rate, coded.astype(f32), decode_lse(coded, lax.rem(head, 2)))


def blend_kernel(rate, offs_any, low, high, found_ref, *refs):
    near, state, offs, sem = refs[:4], refs[4], refs[5], refs[6]
    copy = fetch(offs_any, offs, sem)
    mine = lax.rem(lax.axis_index("seq"), 4)
    for h in range(4):
        state[h, :, :] = (low, high)[h // 2][h % 2, :, :]
    copy.wait()
    for h in range(4):
        new = found_ref[h, :, :]
        absorb(state, h, offs[h, 1], rate, new, spread_lse(new, half_mask(new.shape[0], h % 2)))
    for d in range(4):
        head = mine ^ d
        absorb_coded(state, head, offs[head, 2], rate, near[d][...])


def final_kernel(levels, offs_any, state_in, *refs):
    far, state, out_any, offs, out, sem, sems = refs[:4], refs[4], refs[5], refs[6], refs[7], refs[8], refs[9]
    copy = fetch(offs_any, offs, sem)
    mine = lax.rem(lax.axis_index("seq"), 4)
    copy.wait()
    for d in range(4):
        head = mine ^ d
        at = 0
        for level, count, rate, near in levels:
            if not near:
                absorb_coded(state, head, offs[head, level], rate, far[d][at : at + count, :])
                at += count
    step = SEG
    vl = half_mask(step, 0)
    copies = []
    for i in range(out.shape[0] // step):
        part = slice(i * step, (i + 1) * step)
        for p in range(2):
            out[part, p * LANES : (p + 1) * LANES] = jnp.where(
                vl, state[2 * p, part, :], state[2 * p + 1, part, :]
            ).astype(bf16)
        copies.append(pltpu.make_async_copy(out.at[part, :], out_any.at[part, :], sems.at[i]))
        copies[-1].start()
    for copy in copies:
        copy.wait()


def call(
    body, outs, spaces, scratch=(), flops=0, bytes_moved=0, exps=0, aliases=None, out_spaces="", mib=24
):
    whole = pl.BlockSpec(memory_space=VMEM)
    place = {"v": whole, "a": pl.BlockSpec(memory_space=pltpu.HBM)}
    return pl.pallas_call(
        body,
        out_shape=outs,
        in_specs=[place[c] for c in spaces],
        out_specs=[place[c] for c in out_spaces] if out_spaces else jax.tree.map(lambda _: whole, outs),
        scratch_shapes=list(scratch),
        input_output_aliases=aliases or {},
        compiler_params=pltpu.CompilerParams(vmem_limit_bytes=mib << 20),
        cost_estimate=pl.CostEstimate(flops=flops, bytes_accessed=bytes_moved, transcendentals=exps),
    )


def swapped(shard, bits):
    return lax.ppermute(
        shard, "seq", [(i, i ^ bits) for i in range(lax.axis_size("seq"))]
    )


def per_device(query, key, value, offsets):
    rows, width = query.shape
    places = lax.axis_size("seq")
    rate_three = RATE1 * places // 8
    rate_four = 4 * rate_three
    near_count, mid, top = rows // RATE1, rows // rate_three, rows // rate_four
    levels = (
        (2, near_count, RATE1, True),
        (3, mid, rate_three, False),
        (4, top, rate_four, False),
    )
    offsets = offsets.T
    table = pltpu.SMEM(offsets.shape, jnp.int32)
    one_sem = pltpu.SemaphoreType.DMA

    def tile(n, kind=bf16):
        return jax.ShapeDtypeStruct((n, LANES), kind)

    wide = jax.ShapeDtypeStruct((2, rows, LANES), f32)
    state_shape = jax.ShapeDtypeStruct((4, rows, LANES), f32)
    parts = call(
        lambda *refs: pack_kernel(levels, *refs),
        [tile(near_count * 3 // 2)] * 4
        + [tile((mid + top) * 3 // 2)] * 4
        + [jax.ShapeDtypeStruct(query.shape, bf16)] * 3
        + [wide] * 3,
        "aaaa",
        (table, pltpu.SemaphoreType.DMA((4,))),
        bytes_moved=5 << 20,
        mib=PACK_MIB,
    )(*(pltpu.with_memory_space_constraint(x, pltpu.HBM) for x in (offsets, query, key, value)))
    near_sent, far_sent, narrow, wides = parts[:4], parts[4:8], parts[8:11], parts[11:]
    far_held = [far_sent[0]] + [swapped(far_sent[d], d) for d in (1, 2, 3)]
    near_held = [near_sent[0]] + [swapped(near_sent[d], d) for d in (1, 2, 3)]

    states = [
        call(
            lambda *refs, pair=pair: first_kernel(pair, *refs),
            wide,
            "vvv",
            flops=2 << 30,
            bytes_moved=4 << 20,
            exps=2 << 20,
        )(*narrow)
        for pair in range(2)
    ]

    own_top = jnp.concatenate([r[mid : mid + top] for r in far_held], axis=0)
    other_top = swapped(own_top, 16)
    held = jnp.concatenate([r[:mid] for r in far_held] + [own_top, other_top], axis=0)
    gathered = [held] + [swapped(held, b) for b in (8, 4, 12)]

    near_found = call(
        lambda *refs: near_kernel(near_count, *refs),
        [tile(near_count)] * 4,
        "vvvv",
        flops=6 << 30,
        bytes_moved=2 << 20,
        exps=4 << 20,
    )(*near_held)
    near_back = [near_found[0]] + [swapped(near_found[d], d) for d in (1, 2, 3)]

    found = call(
        lambda *refs: second_kernel(RATE1, *refs),
        jax.ShapeDtypeStruct((4, near_count, LANES), f32),
        "avvv",
        (table, one_sem),
        flops=2 << 30,
        bytes_moved=4 << 20,
        exps=1 << 20,
    )(offsets, *wides)

    far_found = call(
        lambda *refs: far_kernel(mid, top, *refs),
        [tile(mid + top)] * 4,
        "v" * 8,
        flops=2 << 30,
        bytes_moved=2 << 20,
        exps=1 << 20,
    )(*far_held, *gathered)
    far_back = [far_found[0]] + [swapped(far_found[d], d) for d in (1, 2, 3)]

    state = call(
        lambda *refs: blend_kernel(RATE1, *refs),
        state_shape,
        "avvvvvvv",
        (table, one_sem),
        bytes_moved=10 << 20,
    )(offsets, *states, found, *near_back)

    return call(
        lambda *refs: final_kernel(levels, *refs),
        [state_shape, jax.ShapeDtypeStruct((rows, width), bf16)],
        "avvvvv",
        (table, VMEM((rows, width), bf16), one_sem, pltpu.SemaphoreType.DMA((rows // SEG,))),
        bytes_moved=6 << 20,
        aliases={1: 0},
        out_spaces="va",
    )(offsets, state, *far_back)[1]


def solution(mesh):
    return jax.shard_map(
        per_device,
        mesh=mesh,
        in_specs=(P("seq", "head"), P("seq", "head"), P("seq", "head"), P(None, "head")),
        out_specs=P("seq", "head"),
        check_vma=False,
    )
```

```python
import jax
import jax.numpy as jnp
from jax import lax
from jax.experimental import pallas as pl
from jax.experimental.pallas import tpu as pltpu
from jax.sharding import PartitionSpec as P


SEG = 512
PACK_MIB = 24
RATE1 = 4
bf16 = jnp.bfloat16
f32 = jnp.float32
LANES = 128
HALF = 64
VMEM = pltpu.VMEM


def dot_nt(a, b):
    return lax.dot_general(a, b, (((1,), (1,)), ((), ())), preferred_element_type=f32)


def dot_nn(a, b):
    return lax.dot_general(a, b, (((1,), (0,)), ((), ())), preferred_element_type=f32)


def half_mask(rows, half):
    lane = lax.broadcasted_iota(jnp.int32, (rows, LANES), 1)
    return lax.div(lane, HALF) == half


def swap_halves(x):
    return pltpu.roll(x, HALF, 1)


def softmax(scores, values):
    top = scores[0].max(axis=1, keepdims=True)
    for s in scores[1:]:
        top = jnp.maximum(top, s.max(axis=1, keepdims=True))
    probs = [jnp.exp(s - top).astype(bf16) for s in scores]
    return top, jnp.concatenate(probs, axis=1), jnp.concatenate(values, axis=0)


def attend_one(q, keys, values):
    top, probs, wide = softmax([dot_nt(q, k) for k in keys], values)
    acc = dot_nn(probs, wide)
    total = acc[:, LANES:]
    return acc[:, :LANES] / total, top + jnp.log(total)


def attend_pair(queries, keys, values):
    low = half_mask(queries[0].shape[0], 0)
    tops, probs, wides = zip(
        *[softmax([dot_nt(q, k)], [v]) for q, k, v in zip(queries, keys, values)]
    )
    acc = dot_nn(jnp.concatenate(probs, axis=1), jnp.concatenate(wides, axis=0))
    total = acc[:, LANES:]
    return acc[:, :LANES] / total, jnp.where(low, tops[0], tops[1]) + jnp.log(total)


def with_ones(v, vl):
    zero, one = jnp.zeros_like(v), jnp.ones_like(v)
    return jnp.concatenate([jnp.where(vl, v, zero), jnp.where(vl, one, zero)], axis=1)


def encode(out, lse, vl):
    lane = lax.broadcasted_iota(jnp.int32, out.shape, 1)
    spot = lax.rem(lane, HALF)
    first = lse.astype(bf16).astype(f32)
    rest = lse - first
    second = rest.astype(bf16).astype(f32)
    third = rest - second
    coded = jnp.where(spot == 0, first, jnp.where(spot == 1, second, third))
    return jnp.where(vl, out, coded)


def decode_lse(coded, half):
    row = lax.broadcasted_iota(jnp.int32, (LANES, LANES), 0)
    pick = jnp.logical_and(lax.div(row, HALF) != half, lax.rem(row, HALF) < 3)
    return dot_nn(coded, jnp.where(pick, 1.0, 0.0).astype(bf16))


def widen(src, dst):
    rows = src.shape[0]
    step = min(rows, 512)

    @pl.loop(0, rows // step)
    def _(i):
        part = pl.ds(pl.multiple_of(i * step, step), step)
        for p in range(src.shape[1] // LANES):
            dst[p, part, :] = src[part, p * LANES : (p + 1) * LANES].astype(f32)


def fetch(offs_any, offs, sem):
    copy = pltpu.make_async_copy(offs_any, offs, sem)
    copy.start()
    return copy


def pack_kernel(levels, offs_any, q_any, k_any, v_any, *rest):
    near_out, far_out, (qb, kb, vb, qs, ks, vs, offs, sems) = rest[0:4], rest[4:8], rest[8:]
    mine = lax.rem(lax.axis_index("seq"), 4)
    copies = [fetch(k_any, kb, sems.at[0]), fetch(v_any, vb, sems.at[1])]
    copies += [fetch(q_any, qb, sems.at[2]), fetch(offs_any, offs, sems.at[3])]
    for copy, narrow, wide in zip(copies, (kb, vb, qb), (ks, vs, qs)):
        copy.wait()
        widen(narrow, wide)
    copies[3].wait()
    for d in range(4):
        head = mine ^ d
        pair, half = lax.div(head, 2), lax.rem(head, 2)
        base = [0, 0]
        for what in ("kv", "q"):
            for level, count, rate, near in levels:
                off = offs[head, level]
                ref = near_out[d] if near else far_out[d]
                at = base[near]
                if what == "kv":
                    vl = half_mask(count, half)
                    k = ks[pair, pl.ds(off, count, rate), :]
                    v = vs[pair, pl.ds(off, count, rate), :]
                    ref[at : at + count, :] = jnp.where(vl, v, swap_halves(k)).astype(bf16)
                    base[near] = at + count
                else:
                    few = count // 2
                    vl = half_mask(few, half)
                    q_one = qs[pair, pl.ds(off, few, rate), :]
                    q_two = qs[pair, pl.ds(off + few * rate, few, rate), :]
                    tile = jnp.where(vl, q_two, swap_halves(q_one))
                    ref[at : at + few, :] = (tile * 0.125).astype(bf16)
                    base[near] = at + few


def first_kernel(pair, q_ref, k_ref, v_ref, *rest):
    out_ref, lse_ref = rest[-2:]
    scale = jnp.asarray(0.125, bf16)
    cols = slice(pair * LANES, (pair + 1) * LANES)

    @pl.loop(0, q_ref.shape[0] // SEG)
    def _(s):
        part = pl.ds(pl.multiple_of(s * SEG, SEG), SEG)
        q, k, v = q_ref[part, cols] * scale, k_ref[part, cols], v_ref[part, cols]
        halves = [half_mask(SEG, h) for h in range(2)]
        out, lse = attend_pair(
            [q, q],
            [jnp.where(vl, k, jnp.zeros_like(k)) for vl in halves],
            [with_ones(v, vl) for vl in halves],
        )
        out_ref[pair, part, :] = out
        lse_ref[pair, part, :] = lse


def absorb(outs, lses, head, off, rate, new, lse_new):
    pair, half = lax.div(head, 2), lax.rem(head, 2)
    count = new.shape[0]
    vl = half_mask(count, half)
    picked = pl.ds(off, count, rate)
    old, lse_old = outs[pair, picked, :], lses[pair, picked, :]
    gap = lse_new - lse_old
    small = jnp.exp(-jnp.abs(gap))
    share = jnp.where(gap > 0.0, 1.0, small) / (1.0 + small)
    outs[pair, picked, :] = jnp.where(vl, old + share * (new - old), old)
    lse = jnp.maximum(lse_old, lse_new) + jnp.log(1.0 + small)
    lses[pair, picked, :] = jnp.where(vl, lse, lse_old)


def absorb_coded(outs, lses, head, off, rate, coded):
    lse = decode_lse(coded, lax.rem(head, 2))
    absorb(outs, lses, head, off, rate, coded.astype(f32), lse)


def keys_values(tile, half):
    vl = half_mask(tile.shape[0], half)
    zero, one = jnp.zeros_like(tile), jnp.ones_like(tile)
    return jnp.where(vl, zero, tile), jnp.concatenate([jnp.where(vl, tile, zero), one], axis=1)


def near_kernel(count, *refs):
    ins, outs = refs[:4], refs[4:]
    half = lax.rem(lax.axis_index("seq"), 2)
    keys, values = zip(*[keys_values(r[:count, :], half) for r in ins])
    few = count // 2
    vl = half_mask(count, half)
    for d in range(4):
        tile = ins[d][count : count + few, :]
        other = swap_halves(tile.astype(f32)).astype(bf16)
        out, lse = attend_one(jnp.concatenate([tile, other], axis=0), keys, values)
        outs[d][...] = encode(out, lse, vl).astype(bf16)


def far_kernel(mid, top, *refs):
    far, gathered, outs = refs[:4], refs[4:8], refs[8:12]
    half = lax.rem(lax.axis_index("seq"), 2)
    base = mid + top
    blocks = (
        ([r[: 4 * mid, :] for r in gathered], base, mid // 2, 0),
        ([r[4 * mid :, :] for r in gathered], base + mid // 2, top // 2, mid),
    )
    for tiles, q_at, few, out_at in blocks:
        keys, values = zip(*[keys_values(t, half) for t in tiles])
        tile = jnp.concatenate([r[q_at : q_at + few, :].astype(f32) for r in far], axis=0)
        q = jnp.concatenate([tile, swap_halves(tile)], axis=0).astype(bf16)
        out, lse = attend_one(q, keys, values)
        found = encode(out, lse, half_mask(8 * few, half))
        for part in range(2):
            for d in range(4):
                at, start = out_at + part * few, (part * 4 + d) * few
                outs[d][at : at + few, :] = found[start : start + few, :].astype(bf16)


def second_kernel(rate, offs_any, qs, ks, vs, outs_in, lses_in, *refs):
    near, outs, lses, offs, sem = refs[:4], refs[4], refs[5], refs[6], refs[7]
    copy = fetch(offs_any, offs, sem)
    mine = lax.rem(lax.axis_index("seq"), 4)
    count = near[0].shape[0]
    copy.wait()
    for p in range(2):
        queries, keys, values = [], [], []
        for h in range(2):
            vl = half_mask(count, h)
            picked = pl.ds(offs[2 * p + h, 1], count, rate)
            queries.append((qs[p, picked, :] * 0.125).astype(bf16))
            k = ks[p, picked, :]
            keys.append(jnp.where(vl, k, jnp.zeros_like(k)).astype(bf16))
            values.append(with_ones(vs[p, picked, :], vl).astype(bf16))
        out, lse = attend_pair(queries, keys, values)
        for h in range(2):
            head = 2 * p + h
            absorb(outs, lses, head, offs[head, 1], rate, out, lse)
    for d in range(4):
        head = mine ^ d
        absorb_coded(outs, lses, head, offs[head, 2], rate, near[d][...])


def final_kernel(levels, offs_any, outs_in, lses_in, *refs):
    far, outs, lses, out_any = refs[:4], refs[4], refs[5], refs[6]
    offs, out, sem, sems = refs[7:]
    copy = fetch(offs_any, offs, sem)
    mine = lax.rem(lax.axis_index("seq"), 4)
    copy.wait()
    for d in range(4):
        head = mine ^ d
        at = 0
        for level, count, rate, near in levels:
            if not near:
                absorb_coded(outs, lses, head, offs[head, level], rate, far[d][at : at + count, :])
                at += count
    copies = []
    for i in range(out.shape[0] // SEG):
        part = slice(i * SEG, (i + 1) * SEG)
        for p in range(2):
            out[part, p * LANES : (p + 1) * LANES] = outs[p, part, :].astype(bf16)
        copies.append(pltpu.make_async_copy(out.at[part, :], out_any.at[part, :], sems.at[i]))
        copies[-1].start()
    for copy in copies:
        copy.wait()


def call(
    body, outs, spaces, scratch=(), flops=0, bytes_moved=0, exps=0, aliases=None, out_spaces="", mib=24
):
    whole = pl.BlockSpec(memory_space=VMEM)
    place = {"v": whole, "a": pl.BlockSpec(memory_space=pltpu.HBM)}
    return pl.pallas_call(
        body,
        out_shape=outs,
        in_specs=[place[c] for c in spaces],
        out_specs=[place[c] for c in out_spaces] if out_spaces else jax.tree.map(lambda _: whole, outs),
        scratch_shapes=list(scratch),
        input_output_aliases=aliases or {},
        compiler_params=pltpu.CompilerParams(vmem_limit_bytes=mib << 20),
        cost_estimate=pl.CostEstimate(flops=flops, bytes_accessed=bytes_moved, transcendentals=exps),
    )


def swapped(shard, bits):
    return lax.ppermute(
        shard, "seq", [(i, i ^ bits) for i in range(lax.axis_size("seq"))]
    )


def per_device(query, key, value, offsets):
    rows, width = query.shape
    places = lax.axis_size("seq")
    rate_three = RATE1 * places // 8
    rate_four = 4 * rate_three
    near_count, mid, top = rows // RATE1, rows // rate_three, rows // rate_four
    levels = (
        (2, near_count, RATE1, True),
        (3, mid, rate_three, False),
        (4, top, rate_four, False),
    )
    offsets = offsets.T
    table = pltpu.SMEM(offsets.shape, jnp.int32)
    one_sem = pltpu.SemaphoreType.DMA

    def tile(n, kind=bf16):
        return jax.ShapeDtypeStruct((n, LANES), kind)

    wide = jax.ShapeDtypeStruct((2, rows, LANES), f32)
    parts = call(
        lambda *refs: pack_kernel(levels, *refs),
        [tile(near_count * 3 // 2)] * 4
        + [tile((mid + top) * 3 // 2)] * 4
        + [jax.ShapeDtypeStruct(query.shape, bf16)] * 3
        + [wide] * 3,
        "aaaa",
        (table, pltpu.SemaphoreType.DMA((4,))),
        bytes_moved=5 << 20,
        mib=PACK_MIB,
    )(*(pltpu.with_memory_space_constraint(x, pltpu.HBM) for x in (offsets, query, key, value)))
    near_sent, far_sent, narrow, wides = parts[:4], parts[4:8], parts[8:11], parts[11:]
    far_held = [far_sent[0]] + [swapped(far_sent[d], d) for d in (1, 2, 3)]
    near_held = [near_sent[0]] + [swapped(near_sent[d], d) for d in (1, 2, 3)]

    state = ()
    for pair in range(2):
        state = call(
            lambda *refs, pair=pair: first_kernel(pair, *refs),
            [wide, wide],
            "vvv" + "v" * len(state),
            flops=2 << 30,
            bytes_moved=4 << 20,
            exps=2 << 20,
            aliases={3: 0, 4: 1} if state else None,
        )(*narrow, *state)

    own_top = jnp.concatenate([r[mid : mid + top] for r in far_held], axis=0)
    other_top = swapped(own_top, 16)
    held = jnp.concatenate([r[:mid] for r in far_held] + [own_top, other_top], axis=0)
    gathered = [held] + [swapped(held, b) for b in (8, 4, 12)]

    near_found = call(
        lambda *refs: near_kernel(near_count, *refs),
        [tile(near_count)] * 4,
        "vvvv",
        flops=6 << 30,
        bytes_moved=2 << 20,
        exps=4 << 20,
    )(*near_held)
    near_back = [near_found[0]] + [swapped(near_found[d], d) for d in (1, 2, 3)]

    far_found = call(
        lambda *refs: far_kernel(mid, top, *refs),
        [tile(mid + top)] * 4,
        "v" * 8,
        flops=2 << 30,
        bytes_moved=2 << 20,
        exps=1 << 20,
    )(*far_held, *gathered)
    far_back = [far_found[0]] + [swapped(far_found[d], d) for d in (1, 2, 3)]

    state = call(
        lambda *refs: second_kernel(RATE1, *refs),
        [wide, wide],
        "avvvvvvvvv",
        (table, one_sem),
        flops=2 << 30,
        bytes_moved=4 << 20,
        exps=1 << 20,
        aliases={4: 0, 5: 1},
    )(offsets, *wides, *state, *near_back)

    return call(
        lambda *refs: final_kernel(levels, *refs),
        [wide, wide, jax.ShapeDtypeStruct((rows, width), bf16)],
        "avvvvvv",
        (table, VMEM((rows, width), bf16), one_sem, pltpu.SemaphoreType.DMA((rows // SEG,))),
        bytes_moved=6 << 20,
        aliases={1: 0, 2: 1},
        out_spaces="vva",
    )(offsets, *state, *far_back)[2]


def solution(mesh):
    return jax.shard_map(
        per_device,
        mesh=mesh,
        in_specs=(P("seq", "head"), P("seq", "head"), P("seq", "head"), P(None, "head")),
        out_specs=P("seq", "head"),
        check_vma=False,
    )
```

```python
import jax
import jax.numpy as jnp
from jax import lax
from jax.experimental import pallas as pl
from jax.experimental.pallas import tpu as pltpu
from jax.sharding import PartitionSpec as P


SEG = 512
PACK_MIB = 24
RATE1 = 4
bf16 = jnp.bfloat16
f32 = jnp.float32
LANES = 128
HALF = 64
VMEM = pltpu.VMEM


def dot_nt(a, b):
    return lax.dot_general(a, b, (((1,), (1,)), ((), ())), preferred_element_type=f32)


def dot_nn(a, b):
    return lax.dot_general(a, b, (((1,), (0,)), ((), ())), preferred_element_type=f32)


def half_mask(rows, half):
    lane = lax.broadcasted_iota(jnp.int32, (rows, LANES), 1)
    return lax.div(lane, HALF) == half


def swap_halves(x):
    return pltpu.roll(x, HALF, 1)


def softmax(scores, values):
    top = scores[0].max(axis=1, keepdims=True)
    for s in scores[1:]:
        top = jnp.maximum(top, s.max(axis=1, keepdims=True))
    probs = [jnp.exp(s - top).astype(bf16) for s in scores]
    return top, jnp.concatenate(probs, axis=1), jnp.concatenate(values, axis=0)


def attend_one(q, keys, values):
    top, probs, wide = softmax([dot_nt(q, k) for k in keys], values)
    acc = dot_nn(probs, wide)
    total = acc[:, LANES:]
    return acc[:, :LANES] / total, top + jnp.log(total)


def attend_pair(queries, keys, values):
    low = half_mask(queries[0].shape[0], 0)
    tops, probs, wides = zip(
        *[softmax([dot_nt(q, k)], [v]) for q, k, v in zip(queries, keys, values)]
    )
    acc = dot_nn(jnp.concatenate(probs, axis=1), jnp.concatenate(wides, axis=0))
    total = acc[:, LANES:]
    return acc[:, :LANES] / total, jnp.where(low, tops[0], tops[1]) + jnp.log(total)


def with_ones(v, vl):
    zero, one = jnp.zeros_like(v), jnp.ones_like(v)
    return jnp.concatenate([jnp.where(vl, v, zero), jnp.where(vl, one, zero)], axis=1)


def encode(out, lse, vl):
    lane = lax.broadcasted_iota(jnp.int32, out.shape, 1)
    spot = lax.rem(lane, HALF)
    first = lse.astype(bf16).astype(f32)
    rest = lse - first
    second = rest.astype(bf16).astype(f32)
    third = rest - second
    coded = jnp.where(spot == 0, first, jnp.where(spot == 1, second, third))
    return jnp.where(vl, out, coded)


def decode_pair(one, two, odd):
    even = jnp.where(odd == 1, two, one)
    other = jnp.where(odd == 1, one, two)
    low = half_mask(one.shape[0], 0)
    row = lax.broadcasted_iota(jnp.int32, (LANES, LANES), 0)
    column = lax.broadcasted_iota(jnp.int32, (LANES, LANES), 1)
    pick = jnp.logical_and(
        lax.div(row, HALF) != lax.div(column, HALF), lax.rem(row, HALF) < 3
    )
    lse = dot_nn(jnp.where(low, other, even), jnp.where(pick, 1.0, 0.0).astype(bf16))
    return jnp.where(low, even, other).astype(f32), lse


def absorb_pairs(outs, lses, items, rate):
    loaded = []
    for pair, offs, new, lse_new in items:
        count = new.shape[0]
        low = half_mask(count, 0)
        spots = [pl.ds(off, count, rate) for off in offs]
        olds = [outs[pair, spot, :] for spot in spots]
        lse_olds = [lses[pair, spot, :] for spot in spots]
        loaded.append((low, spots, olds, lse_olds))
    merged = []
    for (pair, offs, new, lse_new), (low, spots, olds, lse_olds) in zip(items, loaded):
        old, lse_old = jnp.where(low, *olds), jnp.where(low, *lse_olds)
        gap = lse_new - lse_old
        small = jnp.exp(-jnp.abs(gap))
        share = jnp.where(gap > 0.0, 1.0, small) / (1.0 + small)
        lse = jnp.maximum(lse_old, lse_new) + jnp.log(1.0 + small)
        merged.append((old + share * (new - old), lse))
    for (pair, *_), (low, spots, olds, lse_olds), (out, lse) in zip(items, loaded, merged):
        outs[pair, spots[0], :] = jnp.where(low, out, olds[0])
        lses[pair, spots[0], :] = jnp.where(low, lse, lse_olds[0])
        outs[pair, spots[1], :] = jnp.where(low, outs[pair, spots[1], :], out)
        lses[pair, spots[1], :] = jnp.where(low, lses[pair, spots[1], :], lse)


def absorb_coded(outs, lses, coded, offs, level, rate):
    mine = lax.rem(lax.axis_index("seq"), 4)
    items = []
    for j in range(2):
        pair = lax.div(mine, 2) ^ j
        out, lse = decode_pair(coded[2 * j], coded[2 * j + 1], lax.rem(mine, 2))
        items.append((pair, (offs.of(2 * pair, level), offs.of(2 * pair + 1, level)), out, lse))
    absorb_pairs(outs, lses, items, rate)


def widen(src, dst):
    rows = src.shape[0]
    step = min(rows, 512)

    @pl.loop(0, rows // step)
    def _(i):
        part = pl.ds(pl.multiple_of(i * step, step), step)
        for p in range(src.shape[1] // LANES):
            dst[p, part, :] = src[part, p * LANES : (p + 1) * LANES].astype(f32)


class Table:
    def __init__(self, ref):
        self.rows = ref[...]

    def of(self, head, level):
        if isinstance(head, int):
            return self.rows[head, level]
        found = self.rows[0, level]
        for h in range(1, 4):
            found = jnp.where(head == h, self.rows[h, level], found)
        return found


def fetch(offs_any, offs, sem):
    copy = pltpu.make_async_copy(offs_any, offs, sem)
    copy.start()
    return copy


def pack_kernel(levels, offs_any, q_any, k_any, v_any, *rest):
    near_out, far_out, (qb, kb, vb, qs, ks, vs, offs, sems) = rest[0:4], rest[4:8], rest[8:]
    mine = lax.rem(lax.axis_index("seq"), 4)
    copies = [fetch(k_any, kb, sems.at[0]), fetch(v_any, vb, sems.at[1])]
    copies += [fetch(q_any, qb, sems.at[2]), fetch(offs_any, offs, sems.at[3])]
    for copy, narrow, wide in zip(copies, (kb, vb, qb), (ks, vs, qs)):
        copy.wait()
        widen(narrow, wide)
    copies[3].wait()
    for d in range(4):
        head = mine ^ d
        pair, half = lax.div(head, 2), lax.rem(head, 2)
        base = [0, 0]
        for what in ("kv", "q"):
            for level, count, rate, near in levels:
                off = offs[head, level]
                near = near or what == "q"
                ref = near_out[d] if near else far_out[d]
                at = base[near]
                if what == "kv":
                    vl = half_mask(count, half)
                    k = ks[pair, pl.ds(off, count, rate), :]
                    v = vs[pair, pl.ds(off, count, rate), :]
                    ref[at : at + count, :] = jnp.where(vl, v, swap_halves(k)).astype(bf16)
                    base[near] = at + count
                else:
                    few = count // 2
                    vl = half_mask(few, half)
                    q_one = qs[pair, pl.ds(off, few, rate), :]
                    q_two = qs[pair, pl.ds(off + few * rate, few, rate), :]
                    tile = jnp.where(vl, q_two, swap_halves(q_one))
                    ref[at : at + few, :] = (tile * 0.125).astype(bf16)
                    base[near] = at + few


def first_kernel(pair, q_ref, k_ref, v_ref, *rest):
    out_ref, lse_ref = rest[-2:]
    scale = jnp.asarray(0.125, bf16)
    cols = slice(pair * LANES, (pair + 1) * LANES)

    @pl.loop(0, q_ref.shape[0] // SEG, unroll=4)
    def _(s):
        part = pl.ds(pl.multiple_of(s * SEG, SEG), SEG)
        q, k, v = q_ref[part, cols] * scale, k_ref[part, cols], v_ref[part, cols]
        halves = [half_mask(SEG, h) for h in range(2)]
        out, lse = attend_pair(
            [q, q],
            [jnp.where(vl, k, jnp.zeros_like(k)) for vl in halves],
            [with_ones(v, vl) for vl in halves],
        )
        out_ref[pair, part, :] = out
        lse_ref[pair, part, :] = lse


def keys_values(tile, half):
    vl = half_mask(tile.shape[0], half)
    zero, one = jnp.zeros_like(tile), jnp.ones_like(tile)
    return jnp.where(vl, zero, tile), jnp.concatenate([jnp.where(vl, tile, zero), one], axis=1)


def near_kernel(count, *refs):
    ins, outs = refs[:4], refs[4:]
    half = lax.rem(lax.axis_index("seq"), 2)
    keys, values = zip(*[keys_values(r[:count, :], half) for r in ins])
    few = count // 2
    vl = half_mask(count, half)
    for d in range(4):
        tile = ins[d][count : count + few, :]
        other = swap_halves(tile.astype(f32)).astype(bf16)
        out, lse = attend_one(jnp.concatenate([tile, other], axis=0), keys, values)
        outs[d][...] = encode(out, lse, vl).astype(bf16)


def far_kernel(base, mid, top, *refs):
    held, gathered, outs = refs[:4], refs[4:8], refs[8:12]
    half = lax.rem(lax.axis_index("seq"), 2)
    blocks = (
        ([r[: 4 * mid, :] for r in gathered], base, mid // 2, 0),
        ([r[4 * mid :, :] for r in gathered], base + mid // 2, top // 2, mid),
    )
    for tiles, q_at, few, out_at in blocks:
        keys, values = zip(*[keys_values(t, half) for t in tiles])
        tile = jnp.concatenate([r[q_at : q_at + few, :].astype(f32) for r in held], axis=0)
        q = jnp.concatenate([tile, swap_halves(tile)], axis=0).astype(bf16)
        out, lse = attend_one(q, keys, values)
        found = encode(out, lse, half_mask(8 * few, half))
        for part in range(2):
            for d in range(4):
                at, start = out_at + part * few, (part * 4 + d) * few
                outs[d][at : at + few, :] = found[start : start + few, :].astype(bf16)


def second_kernel(rate, offs_ref, qs, ks, vs, outs_in, lses_in, *refs):
    near, outs, lses = refs[:4], refs[4], refs[5]
    offs = Table(offs_ref)
    count = near[0].shape[0]
    for p in range(2):
        queries, keys, values = [], [], []
        for h in range(2):
            vl = half_mask(count, h)
            picked = pl.ds(offs.of(2 * p + h, 1), count, rate)
            queries.append((qs[p, picked, :] * 0.125).astype(bf16))
            k = ks[p, picked, :]
            keys.append(jnp.where(vl, k, jnp.zeros_like(k)).astype(bf16))
            values.append(with_ones(vs[p, picked, :], vl).astype(bf16))
        out, lse = attend_pair(queries, keys, values)
        absorb_pairs(outs, lses, [(p, (offs.of(2 * p, 1), offs.of(2 * p + 1, 1)), out, lse)], rate)
    absorb_coded(outs, lses, [r[...] for r in near], offs, 2, rate)


def final_kernel(levels, offs_ref, outs_in, lses_in, *refs):
    far, outs, lses, out_any = refs[:4], refs[4], refs[5], refs[6]
    out, sems = refs[7:]
    offs = Table(offs_ref)
    at = 0
    for level, count, rate, near in levels:
        if not near:
            absorb_coded(outs, lses, [r[at : at + count, :] for r in far], offs, level, rate)
            at += count
    copies = []
    for i in range(out.shape[0] // SEG):
        part = slice(i * SEG, (i + 1) * SEG)
        for p in range(2):
            out[part, p * LANES : (p + 1) * LANES] = outs[p, part, :].astype(bf16)
        copies.append(pltpu.make_async_copy(out.at[part, :], out_any.at[part, :], sems.at[i]))
        copies[-1].start()
    for copy in copies:
        copy.wait()


def call(
    body, outs, spaces, scratch=(), flops=0, bytes_moved=0, exps=0, aliases=None, out_spaces="", mib=24
):
    whole = pl.BlockSpec(memory_space=VMEM)
    place = {"v": whole, "a": pl.BlockSpec(memory_space=pltpu.HBM), "s": pl.BlockSpec(memory_space=pltpu.SMEM)}
    return pl.pallas_call(
        body,
        out_shape=outs,
        in_specs=[place[c] for c in spaces],
        out_specs=[place[c] for c in out_spaces] if out_spaces else jax.tree.map(lambda _: whole, outs),
        scratch_shapes=list(scratch),
        input_output_aliases=aliases or {},
        compiler_params=pltpu.CompilerParams(vmem_limit_bytes=mib << 20),
        cost_estimate=pl.CostEstimate(flops=flops, bytes_accessed=bytes_moved, transcendentals=exps),
    )


def swapped(shard, bits):
    return lax.ppermute(
        shard, "seq", [(i, i ^ bits) for i in range(lax.axis_size("seq"))]
    )


def per_device(query, key, value, offsets):
    rows, width = query.shape
    places = lax.axis_size("seq")
    rate_three = RATE1 * places // 8
    rate_four = 4 * rate_three
    near_count, mid, top = rows // RATE1, rows // rate_three, rows // rate_four
    levels = (
        (2, near_count, RATE1, True),
        (3, mid, rate_three, False),
        (4, top, rate_four, False),
    )
    queries = (near_count + mid + top) // 2
    offsets = offsets.T
    table = pltpu.SMEM(offsets.shape, jnp.int32)

    def tile(n, kind=bf16):
        return jax.ShapeDtypeStruct((n, LANES), kind)

    wide = jax.ShapeDtypeStruct((2, rows, LANES), f32)
    parts = call(
        lambda *refs: pack_kernel(levels, *refs),
        [tile(near_count + queries)] * 4
        + [tile(mid + top)] * 4
        + [jax.ShapeDtypeStruct(query.shape, bf16)] * 3
        + [wide] * 3,
        "aaaa",
        (table, pltpu.SemaphoreType.DMA((4,))),
        bytes_moved=5 << 20,
        mib=PACK_MIB,
    )(*(pltpu.with_memory_space_constraint(x, pltpu.HBM) for x in (offsets, query, key, value)))
    near_sent, far_sent, narrow, wides = parts[:4], parts[4:8], parts[8:11], parts[11:]
    far_held = [far_sent[0]] + [swapped(far_sent[d], d) for d in (1, 2, 3)]
    near_held = [near_sent[0]] + [swapped(near_sent[d], d) for d in (1, 2, 3)]

    state = ()
    for pair in range(2):
        state = call(
            lambda *refs, pair=pair: first_kernel(pair, *refs),
            [wide, wide],
            "vvv" + "v" * len(state),
            flops=2 << 30,
            bytes_moved=4 << 20,
            exps=2 << 20,
            aliases={3: 0, 4: 1} if state else None,
        )(*narrow, *state)

    own_top = jnp.concatenate([r[mid : mid + top] for r in far_held], axis=0)
    other_top = swapped(own_top, 16)
    held = jnp.concatenate([r[:mid] for r in far_held] + [own_top, other_top], axis=0)
    gathered = [held] + [swapped(held, b) for b in (8, 4, 12)]

    near_found = call(
        lambda *refs: near_kernel(near_count, *refs),
        [tile(near_count)] * 4,
        "vvvv",
        flops=6 << 30,
        bytes_moved=2 << 20,
        exps=4 << 20,
    )(*near_held)
    near_back = [near_found[0]] + [swapped(near_found[d], d) for d in (1, 2, 3)]

    far_found = call(
        lambda *refs: far_kernel(near_count * 3 // 2, mid, top, *refs),
        [tile(mid + top)] * 4,
        "v" * 8,
        flops=2 << 30,
        bytes_moved=2 << 20,
        exps=1 << 20,
    )(*near_held, *gathered)
    far_back = [far_found[0]] + [swapped(far_found[d], d) for d in (1, 2, 3)]

    state = call(
        lambda *refs: second_kernel(RATE1, *refs),
        [wide, wide],
        "vvvvvvvvvv",
        flops=2 << 30,
        bytes_moved=4 << 20,
        exps=1 << 20,
        aliases={4: 0, 5: 1},
    )(offsets, *wides, *state, *near_back)

    return call(
        lambda *refs: final_kernel(levels, *refs),
        [wide, wide, jax.ShapeDtypeStruct((rows, width), bf16)],
        "vvvvvvv",
        (VMEM((rows, width), bf16), pltpu.SemaphoreType.DMA((rows // SEG,))),
        bytes_moved=6 << 20,
        aliases={1: 0, 2: 1},
        out_spaces="vva",
    )(offsets, *state, *far_back)[2]


def solution(mesh):
    return jax.shard_map(
        per_device,
        mesh=mesh,
        in_specs=(P("seq", "head"), P("seq", "head"), P("seq", "head"), P(None, "head")),
        out_specs=P("seq", "head"),
        check_vma=False,
    )
```

```python
import jax
import jax.numpy as jnp
from jax import lax
from jax.experimental import pallas as pl
from jax.experimental.pallas import tpu as pltpu
from jax.sharding import PartitionSpec as P


SEG = 512
PACK_MIB = 24
RATE1 = 4
SAFE = 46.0
bf16 = jnp.bfloat16
f32 = jnp.float32
LANES = 128
HALF = 64
VMEM = pltpu.VMEM


def dot_nt(a, b):
    return lax.dot_general(a, b, (((1,), (1,)), ((), ())), preferred_element_type=f32)


def dot_nn(a, b):
    return lax.dot_general(a, b, (((1,), (0,)), ((), ())), preferred_element_type=f32)


def half_mask(rows, half):
    lane = lax.broadcasted_iota(jnp.int32, (rows, LANES), 1)
    return lax.div(lane, HALF) == half


def swap_halves(x):
    return pltpu.roll(x, HALF, 1)


def softmax(scores, values, shift):
    top = None
    if shift:
        top = scores[0].max(axis=1, keepdims=True)
        for s in scores[1:]:
            top = jnp.maximum(top, s.max(axis=1, keepdims=True))
        scores = [s - top for s in scores]
    probs = [jnp.exp(s).astype(bf16) for s in scores]
    return top, jnp.concatenate(probs, axis=1), jnp.concatenate(values, axis=0)


def attend_one(q, keys, values, shift):
    top, probs, wide = softmax([dot_nt(q, k) for k in keys], values, shift)
    acc = dot_nn(probs, wide)
    total = acc[:, LANES:]
    lse = jnp.log(total)
    return acc[:, :LANES] / total, top + lse if shift else lse


def attend_pair(queries, keys, values, shift):
    low = half_mask(queries[0].shape[0], 0)
    tops, probs, wides = zip(
        *[softmax([dot_nt(q, k)], [v], shift) for q, k, v in zip(queries, keys, values)]
    )
    acc = dot_nn(jnp.concatenate(probs, axis=1), jnp.concatenate(wides, axis=0))
    total = acc[:, LANES:]
    lse = jnp.log(total)
    return acc[:, :LANES] / total, jnp.where(low, *tops) + lse if shift else lse


def out_of_range(lse):
    return jnp.where(jnp.abs(lse) < SAFE, 0.0, 1.0).max(axis=0, keepdims=True)


def with_fallback(run):
    flags = run(False)
    worst = flags[0]
    for flag in flags[1:]:
        worst = jnp.maximum(worst, flag)

    @pl.when(jnp.max(worst) > 0.0)
    def _():
        run(True)


def with_ones(v, vl):
    zero, one = jnp.zeros_like(v), jnp.ones_like(v)
    return jnp.concatenate([jnp.where(vl, v, zero), jnp.where(vl, one, zero)], axis=1)


def encode(out, lse, vl):
    lane = lax.broadcasted_iota(jnp.int32, out.shape, 1)
    spot = lax.rem(lane, HALF)
    first = lse.astype(bf16).astype(f32)
    rest = lse - first
    second = rest.astype(bf16).astype(f32)
    third = rest - second
    coded = jnp.where(spot == 0, first, jnp.where(spot == 1, second, third))
    return jnp.where(vl, out, coded)


def decode_pair(one, two, odd):
    even = jnp.where(odd == 1, two, one)
    other = jnp.where(odd == 1, one, two)
    low = half_mask(one.shape[0], 0)
    row = lax.broadcasted_iota(jnp.int32, (LANES, LANES), 0)
    column = lax.broadcasted_iota(jnp.int32, (LANES, LANES), 1)
    pick = jnp.logical_and(
        lax.div(row, HALF) != lax.div(column, HALF), lax.rem(row, HALF) < 3
    )
    lse = dot_nn(jnp.where(low, other, even), jnp.where(pick, 1.0, 0.0).astype(bf16))
    return jnp.where(low, even, other).astype(f32), lse


def absorb_pairs(outs, lses, items, rate):
    loaded = []
    for pair, offs, new, lse_new in items:
        count = new.shape[0]
        low = half_mask(count, 0)
        spots = [pl.ds(off, count, rate) for off in offs]
        olds = [outs[pair, spot, :] for spot in spots]
        lse_olds = [lses[pair, spot, :] for spot in spots]
        loaded.append((low, spots, olds, lse_olds))
    merged = []
    for (pair, offs, new, lse_new), (low, spots, olds, lse_olds) in zip(items, loaded):
        old, lse_old = jnp.where(low, *olds), jnp.where(low, *lse_olds)
        gap = lse_new - lse_old
        small = jnp.exp(-jnp.abs(gap))
        share = jnp.where(gap > 0.0, 1.0, small) / (1.0 + small)
        lse = jnp.maximum(lse_old, lse_new) + jnp.log(1.0 + small)
        merged.append((old + share * (new - old), lse))
    for (pair, *_), (low, spots, olds, lse_olds), (out, lse) in zip(items, loaded, merged):
        outs[pair, spots[0], :] = jnp.where(low, out, olds[0])
        lses[pair, spots[0], :] = jnp.where(low, lse, lse_olds[0])
        outs[pair, spots[1], :] = jnp.where(low, outs[pair, spots[1], :], out)
        lses[pair, spots[1], :] = jnp.where(low, lses[pair, spots[1], :], lse)


def absorb_coded(outs, lses, coded, offs, level, rate):
    mine = lax.rem(lax.axis_index("seq"), 4)
    items = []
    for j in range(2):
        pair = lax.div(mine, 2) ^ j
        out, lse = decode_pair(coded[2 * j], coded[2 * j + 1], lax.rem(mine, 2))
        items.append((pair, (offs.of(2 * pair, level), offs.of(2 * pair + 1, level)), out, lse))
    absorb_pairs(outs, lses, items, rate)


def widen(src, dst):
    rows = src.shape[0]
    step = min(rows, 512)

    @pl.loop(0, rows // step)
    def _(i):
        part = pl.ds(pl.multiple_of(i * step, step), step)
        for p in range(src.shape[1] // LANES):
            dst[p, part, :] = src[part, p * LANES : (p + 1) * LANES].astype(f32)


class Table:
    def __init__(self, ref):
        self.rows = ref[...]

    def of(self, head, level):
        if isinstance(head, int):
            return self.rows[head, level]
        found = self.rows[0, level]
        for h in range(1, 4):
            found = jnp.where(head == h, self.rows[h, level], found)
        return found


def fetch(offs_any, offs, sem):
    copy = pltpu.make_async_copy(offs_any, offs, sem)
    copy.start()
    return copy


def pack_kernel(levels, offs_any, q_any, k_any, v_any, *rest):
    near_out, far_out, (qb, kb, vb, qs, ks, vs, offs, sems) = rest[0:4], rest[4:8], rest[8:]
    mine = lax.rem(lax.axis_index("seq"), 4)
    copies = [fetch(k_any, kb, sems.at[0]), fetch(v_any, vb, sems.at[1])]
    copies += [fetch(q_any, qb, sems.at[2]), fetch(offs_any, offs, sems.at[3])]
    for copy, narrow, wide in zip(copies, (kb, vb, qb), (ks, vs, qs)):
        copy.wait()
        widen(narrow, wide)
    copies[3].wait()
    for d in range(4):
        head = mine ^ d
        pair, half = lax.div(head, 2), lax.rem(head, 2)
        base = [0, 0]
        for what in ("kv", "q"):
            for level, count, rate, near in levels:
                off = offs[head, level]
                near = near or what == "q"
                ref = near_out[d] if near else far_out[d]
                at = base[near]
                if what == "kv":
                    vl = half_mask(count, half)
                    k = ks[pair, pl.ds(off, count, rate), :]
                    v = vs[pair, pl.ds(off, count, rate), :]
                    ref[at : at + count, :] = jnp.where(vl, v, swap_halves(k)).astype(bf16)
                    base[near] = at + count
                else:
                    few = count // 2
                    vl = half_mask(few, half)
                    q_one = qs[pair, pl.ds(off, few, rate), :]
                    q_two = qs[pair, pl.ds(off + few * rate, few, rate), :]
                    tile = jnp.where(vl, q_two, swap_halves(q_one))
                    ref[at : at + few, :] = (tile * 0.125).astype(bf16)
                    base[near] = at + few


def first_kernel(pair, q_ref, k_ref, v_ref, *rest):
    out_ref, lse_ref = rest[-2:]
    scale = jnp.asarray(0.125, bf16)
    cols = slice(pair * LANES, (pair + 1) * LANES)

    def segment(part, shift):
        q, k, v = q_ref[part, cols] * scale, k_ref[part, cols], v_ref[part, cols]
        halves = [half_mask(SEG, h) for h in range(2)]
        out, lse = attend_pair(
            [q, q],
            [jnp.where(vl, k, jnp.zeros_like(k)) for vl in halves],
            [with_ones(v, vl) for vl in halves],
            shift,
        )
        out_ref[pair, part, :] = out
        lse_ref[pair, part, :] = lse
        return out_of_range(lse)

    def run(shift):
        segments = q_ref.shape[0] // SEG
        if not shift:
            return [segment(slice(i * SEG, (i + 1) * SEG), False) for i in range(segments)]

        @pl.loop(0, segments)
        def _(i):
            segment(pl.ds(pl.multiple_of(i * SEG, SEG), SEG), True)

    with_fallback(run)


def keys_values(tile, half):
    vl = half_mask(tile.shape[0], half)
    zero, one = jnp.zeros_like(tile), jnp.ones_like(tile)
    return jnp.where(vl, zero, tile), jnp.concatenate([jnp.where(vl, tile, zero), one], axis=1)


def near_kernel(count, *refs):
    ins, outs = refs[:4], refs[4:]
    half = lax.rem(lax.axis_index("seq"), 2)
    keys, values = zip(*[keys_values(r[:count, :], half) for r in ins])
    few = count // 2
    vl = half_mask(count, half)

    def run(shift):
        flags = []
        for d in range(4):
            tile = ins[d][count : count + few, :]
            other = swap_halves(tile.astype(f32)).astype(bf16)
            out, lse = attend_one(jnp.concatenate([tile, other], axis=0), keys, values, shift)
            outs[d][...] = encode(out, lse, vl).astype(bf16)
            flags.append(out_of_range(lse))
        return flags

    with_fallback(run)


def far_kernel(base, mid, top, *refs):
    held, gathered, outs = refs[:4], refs[4:8], refs[8:12]
    half = lax.rem(lax.axis_index("seq"), 2)
    blocks = (
        ([r[: 4 * mid, :] for r in gathered], base, mid // 2, 0),
        ([r[4 * mid :, :] for r in gathered], base + mid // 2, top // 2, mid),
    )

    def run(shift):
        flags = []
        for tiles, q_at, few, out_at in blocks:
            keys, values = zip(*[keys_values(t, half) for t in tiles])
            tile = jnp.concatenate([r[q_at : q_at + few, :].astype(f32) for r in held], axis=0)
            q = jnp.concatenate([tile, swap_halves(tile)], axis=0).astype(bf16)
            out, lse = attend_one(q, keys, values, shift)
            found = encode(out, lse, half_mask(8 * few, half))
            for part in range(2):
                for d in range(4):
                    at, start = out_at + part * few, (part * 4 + d) * few
                    outs[d][at : at + few, :] = found[start : start + few, :].astype(bf16)
            flags.append(out_of_range(lse))
        return flags

    with_fallback(run)


def second_kernel(rate, offs_ref, qs, ks, vs, outs_in, lses_in, *refs):
    near, outs, lses = refs[:4], refs[4], refs[5]
    offs = Table(offs_ref)
    count = near[0].shape[0]
    for p in range(2):
        queries, keys, values = [], [], []
        for h in range(2):
            vl = half_mask(count, h)
            picked = pl.ds(offs.of(2 * p + h, 1), count, rate)
            queries.append((qs[p, picked, :] * 0.125).astype(bf16))
            k = ks[p, picked, :]
            keys.append(jnp.where(vl, k, jnp.zeros_like(k)).astype(bf16))
            values.append(with_ones(vs[p, picked, :], vl).astype(bf16))
        out, lse = attend_pair(queries, keys, values, True)
        absorb_pairs(outs, lses, [(p, (offs.of(2 * p, 1), offs.of(2 * p + 1, 1)), out, lse)], rate)
    absorb_coded(outs, lses, [r[...] for r in near], offs, 2, rate)


def final_kernel(levels, offs_ref, outs_in, lses_in, *refs):
    far, outs, lses, out_any = refs[:4], refs[4], refs[5], refs[6]
    out, sems = refs[7:]
    offs = Table(offs_ref)
    at = 0
    for level, count, rate, near in levels:
        if not near:
            absorb_coded(outs, lses, [r[at : at + count, :] for r in far], offs, level, rate)
            at += count
    copies = []
    for i in range(out.shape[0] // SEG):
        part = slice(i * SEG, (i + 1) * SEG)
        for p in range(2):
            out[part, p * LANES : (p + 1) * LANES] = outs[p, part, :].astype(bf16)
        copies.append(pltpu.make_async_copy(out.at[part, :], out_any.at[part, :], sems.at[i]))
        copies[-1].start()
    for copy in copies:
        copy.wait()


def call(
    body, outs, spaces, scratch=(), flops=0, bytes_moved=0, exps=0, aliases=None, out_spaces="", mib=24
):
    whole = pl.BlockSpec(memory_space=VMEM)
    place = {"v": whole, "a": pl.BlockSpec(memory_space=pltpu.HBM), "s": pl.BlockSpec(memory_space=pltpu.SMEM)}
    return pl.pallas_call(
        body,
        out_shape=outs,
        in_specs=[place[c] for c in spaces],
        out_specs=[place[c] for c in out_spaces] if out_spaces else jax.tree.map(lambda _: whole, outs),
        scratch_shapes=list(scratch),
        input_output_aliases=aliases or {},
        compiler_params=pltpu.CompilerParams(vmem_limit_bytes=mib << 20),
        cost_estimate=pl.CostEstimate(flops=flops, bytes_accessed=bytes_moved, transcendentals=exps),
    )


def swapped(shard, bits):
    return lax.ppermute(
        shard, "seq", [(i, i ^ bits) for i in range(lax.axis_size("seq"))]
    )


def per_device(query, key, value, offsets):
    rows, width = query.shape
    places = lax.axis_size("seq")
    rate_three = RATE1 * places // 8
    rate_four = 4 * rate_three
    near_count, mid, top = rows // RATE1, rows // rate_three, rows // rate_four
    levels = (
        (2, near_count, RATE1, True),
        (3, mid, rate_three, False),
        (4, top, rate_four, False),
    )
    queries = (near_count + mid + top) // 2
    offsets = offsets.T
    table = pltpu.SMEM(offsets.shape, jnp.int32)

    def tile(n, kind=bf16):
        return jax.ShapeDtypeStruct((n, LANES), kind)

    wide = jax.ShapeDtypeStruct((2, rows, LANES), f32)
    parts = call(
        lambda *refs: pack_kernel(levels, *refs),
        [tile(near_count + queries)] * 4
        + [tile(mid + top)] * 4
        + [jax.ShapeDtypeStruct(query.shape, bf16)] * 3
        + [wide] * 3,
        "aaaa",
        (table, pltpu.SemaphoreType.DMA((4,))),
        bytes_moved=5 << 20,
        mib=PACK_MIB,
    )(*(pltpu.with_memory_space_constraint(x, pltpu.HBM) for x in (offsets, query, key, value)))
    near_sent, far_sent, narrow, wides = parts[:4], parts[4:8], parts[8:11], parts[11:]
    far_held = [far_sent[0]] + [swapped(far_sent[d], d) for d in (1, 2, 3)]
    near_held = [near_sent[0]] + [swapped(near_sent[d], d) for d in (1, 2, 3)]

    state = ()
    for pair in range(2):
        state = call(
            lambda *refs, pair=pair: first_kernel(pair, *refs),
            [wide, wide],
            "vvv" + "v" * len(state),
            flops=2 << 30,
            bytes_moved=4 << 20,
            exps=2 << 20,
            aliases={3: 0, 4: 1} if state else None,
        )(*narrow, *state)

    own_top = jnp.concatenate([r[mid : mid + top] for r in far_held], axis=0)
    other_top = swapped(own_top, 16)
    held = jnp.concatenate([r[:mid] for r in far_held] + [own_top, other_top], axis=0)
    gathered = [held] + [swapped(held, b) for b in (8, 4, 12)]

    near_found = call(
        lambda *refs: near_kernel(near_count, *refs),
        [tile(near_count)] * 4,
        "vvvv",
        flops=6 << 30,
        bytes_moved=2 << 20,
        exps=4 << 20,
    )(*near_held)
    near_back = [near_found[0]] + [swapped(near_found[d], d) for d in (1, 2, 3)]

    far_found = call(
        lambda *refs: far_kernel(near_count * 3 // 2, mid, top, *refs),
        [tile(mid + top)] * 4,
        "v" * 8,
        flops=2 << 30,
        bytes_moved=2 << 20,
        exps=1 << 20,
    )(*near_held, *gathered)
    far_back = [far_found[0]] + [swapped(far_found[d], d) for d in (1, 2, 3)]

    state = call(
        lambda *refs: second_kernel(RATE1, *refs),
        [wide, wide],
        "vvvvvvvvvv",
        flops=2 << 30,
        bytes_moved=4 << 20,
        exps=1 << 20,
        aliases={4: 0, 5: 1},
    )(offsets, *wides, *state, *near_back)

    return call(
        lambda *refs: final_kernel(levels, *refs),
        [wide, wide, jax.ShapeDtypeStruct((rows, width), bf16)],
        "vvvvvvv",
        (VMEM((rows, width), bf16), pltpu.SemaphoreType.DMA((rows // SEG,))),
        bytes_moved=6 << 20,
        aliases={1: 0, 2: 1},
        out_spaces="vva",
    )(offsets, *state, *far_back)[2]


def solution(mesh):
    return jax.shard_map(
        per_device,
        mesh=mesh,
        in_specs=(P("seq", "head"), P("seq", "head"), P("seq", "head"), P(None, "head")),
        out_specs=P("seq", "head"),
        check_vma=False,
    )
```

```python
import jax
import jax.numpy as jnp
from jax import lax
from jax.experimental import pallas as pl
from jax.experimental.pallas import tpu as pltpu
from jax.sharding import PartitionSpec as P


SEG = 512
PACK_MIB = 24
RATE1 = 4
SAFE = 46.0
FAR = (0, 1, 8, 9)
bf16 = jnp.bfloat16
f32 = jnp.float32
LANES = 128
HALF = 64
VMEM = pltpu.VMEM


def dot_nt(a, b):
    return lax.dot_general(a, b, (((1,), (1,)), ((), ())), preferred_element_type=f32)


def dot_nn(a, b):
    return lax.dot_general(a, b, (((1,), (0,)), ((), ())), preferred_element_type=f32)


def half_mask(rows, half):
    lane = lax.broadcasted_iota(jnp.int32, (rows, LANES), 1)
    return lax.div(lane, HALF) == half


def swap_halves(x):
    return pltpu.roll(x, HALF, 1)


def softmax(scores, values, shift):
    top = None
    if shift:
        top = scores[0].max(axis=1, keepdims=True)
        for s in scores[1:]:
            top = jnp.maximum(top, s.max(axis=1, keepdims=True))
        scores = [s - top for s in scores]
    probs = [jnp.exp(s).astype(bf16) for s in scores]
    return top, jnp.concatenate(probs, axis=1), jnp.concatenate(values, axis=0)


def attend_one(q, keys, values, shift):
    top, probs, wide = softmax([dot_nt(q, k) for k in keys], values, shift)
    acc = dot_nn(probs, wide)
    total = acc[:, LANES:]
    lse = jnp.log(total)
    return acc[:, :LANES] / total, top + lse if shift else lse


def attend_pair(queries, keys, values, shift):
    low = half_mask(queries[0].shape[0], 0)
    tops, probs, wides = zip(
        *[softmax([dot_nt(q, k)], [v], shift) for q, k, v in zip(queries, keys, values)]
    )
    acc = dot_nn(jnp.concatenate(probs, axis=1), jnp.concatenate(wides, axis=0))
    total = acc[:, LANES:]
    lse = jnp.log(total)
    return acc[:, :LANES] / total, jnp.where(low, *tops) + lse if shift else lse


def out_of_range(lse):
    return jnp.where(jnp.abs(lse) < SAFE, 0.0, 1.0).max(axis=0, keepdims=True)


def with_fallback(run):
    flags = run(False)
    worst = flags[0]
    for flag in flags[1:]:
        worst = jnp.maximum(worst, flag)

    @pl.when(jnp.max(worst) > 0.0)
    def _():
        run(True)


def with_ones(v, vl):
    zero, one = jnp.zeros_like(v), jnp.ones_like(v)
    return jnp.concatenate([jnp.where(vl, v, zero), jnp.where(vl, one, zero)], axis=1)


def encode(out, lse, vl):
    lane = lax.broadcasted_iota(jnp.int32, out.shape, 1)
    spot = lax.rem(lane, HALF)
    first = lse.astype(bf16).astype(f32)
    rest = lse - first
    second = rest.astype(bf16).astype(f32)
    third = rest - second
    coded = jnp.where(spot == 0, first, jnp.where(spot == 1, second, third))
    return jnp.where(vl, out, coded)


def decode_pair(one, two, odd):
    even = jnp.where(odd == 1, two, one)
    other = jnp.where(odd == 1, one, two)
    low = half_mask(one.shape[0], 0)
    row = lax.broadcasted_iota(jnp.int32, (LANES, LANES), 0)
    column = lax.broadcasted_iota(jnp.int32, (LANES, LANES), 1)
    pick = jnp.logical_and(
        lax.div(row, HALF) != lax.div(column, HALF), lax.rem(row, HALF) < 3
    )
    lse = dot_nn(jnp.where(low, other, even), jnp.where(pick, 1.0, 0.0).astype(bf16))
    return jnp.where(low, even, other).astype(f32), lse


def absorb_pairs(outs, lses, items, rate):
    loaded = []
    for pair, offs, new, lse_new in items:
        count = new.shape[0]
        low = half_mask(count, 0)
        spots = [pl.ds(off, count, rate) for off in offs]
        olds = [outs[pair, spot, :] for spot in spots]
        lse_olds = [lses[pair, spot, :] for spot in spots]
        loaded.append((low, spots, olds, lse_olds))
    merged = []
    for (pair, offs, new, lse_new), (low, spots, olds, lse_olds) in zip(items, loaded):
        old, lse_old = jnp.where(low, *olds), jnp.where(low, *lse_olds)
        gap = lse_new - lse_old
        small = jnp.exp(-jnp.abs(gap))
        share = jnp.where(gap > 0.0, 1.0, small) / (1.0 + small)
        lse = jnp.maximum(lse_old, lse_new) + jnp.log(1.0 + small)
        merged.append((old + share * (new - old), lse))
    for (pair, *_), (low, spots, olds, lse_olds), (out, lse) in zip(items, loaded, merged):
        outs[pair, spots[0], :] = jnp.where(low, out, olds[0])
        lses[pair, spots[0], :] = jnp.where(low, lse, lse_olds[0])
        outs[pair, spots[1], :] = jnp.where(low, outs[pair, spots[1], :], out)
        lses[pair, spots[1], :] = jnp.where(low, lses[pair, spots[1], :], lse)


def absorb_coded(outs, lses, coded, offs, level, rate, mine):
    items = []
    for j in range(2):
        pair = lax.div(mine, 2) ^ j
        out, lse = decode_pair(coded[2 * j], coded[2 * j + 1], lax.rem(mine, 2))
        items.append((pair, (offs.of(2 * pair, level), offs.of(2 * pair + 1, level)), out, lse))
    absorb_pairs(outs, lses, items, rate)


def widen(src, dst):
    rows = src.shape[0]
    step = min(rows, 512)

    @pl.loop(0, rows // step)
    def _(i):
        part = pl.ds(pl.multiple_of(i * step, step), step)
        for p in range(src.shape[1] // LANES):
            dst[p, part, :] = src[part, p * LANES : (p + 1) * LANES].astype(f32)


class Table:
    def __init__(self, ref):
        self.rows = ref[...]

    def of(self, head, level):
        if isinstance(head, int):
            return self.rows[head, level]
        found = self.rows[0, level]
        for h in range(1, 4):
            found = jnp.where(head == h, self.rows[h, level], found)
        return found


def fetch(offs_any, offs, sem):
    copy = pltpu.make_async_copy(offs_any, offs, sem)
    copy.start()
    return copy


def near_place():
    return lax.rem(lax.axis_index("seq"), 4)


def far_place():
    index = lax.axis_index("seq")
    return lax.rem(index, 2) + 2 * lax.rem(lax.div(index, 8), 2)


def pack_kernel(levels, offs_any, q_any, k_any, v_any, *rest):
    near_out, far_out, (qb, kb, vb, qs, ks, vs, offs, sems) = rest[0:4], rest[4:8], rest[8:]
    copies = [fetch(offs_any, offs, sems.at[3]), fetch(k_any, kb, sems.at[0])]
    copies += [fetch(v_any, vb, sems.at[1]), fetch(q_any, qb, sems.at[2])]
    copies[1].wait()
    widen(kb, ks)
    copies[2].wait()
    widen(vb, vs)
    copies[0].wait()
    groups = ((far_place(), far_out, levels[1:]), (near_place(), near_out, levels[:1]))
    ends = []
    for mine, outs, group in groups:
        for d in range(4):
            head = mine ^ d
            pair, half = lax.div(head, 2), lax.rem(head, 2)
            at = 0
            for level, count, rate in group:
                picked = pl.ds(offs[head, level], count, rate)
                vl = half_mask(count, half)
                tile = jnp.where(vl, vs[pair, picked, :], swap_halves(ks[pair, picked, :]))
                outs[d][at : at + count, :] = tile.astype(bf16)
                at += count
            ends.append(at)
    copies[3].wait()
    widen(qb, qs)
    for (mine, outs, group), end in zip(groups, ends[::4]):
        for d in range(4):
            head = mine ^ d
            pair, half = lax.div(head, 2), lax.rem(head, 2)
            at = end
            for level, count, rate in group:
                off, few = offs[head, level], count // 2
                q_one = qs[pair, pl.ds(off, few, rate), :]
                q_two = qs[pair, pl.ds(off + few * rate, few, rate), :]
                tile = jnp.where(half_mask(few, half), q_two, swap_halves(q_one))
                outs[d][at : at + few, :] = (tile * 0.125).astype(bf16)
                at += few


def first_kernel(pair, q_ref, k_ref, v_ref, *rest):
    out_ref, lse_ref = rest[-2:]
    scale = jnp.asarray(0.125, bf16)
    cols = slice(pair * LANES, (pair + 1) * LANES)

    def segment(part, shift):
        q, k, v = q_ref[part, cols] * scale, k_ref[part, cols], v_ref[part, cols]
        halves = [half_mask(SEG, h) for h in range(2)]
        out, lse = attend_pair(
            [q, q],
            [jnp.where(vl, k, jnp.zeros_like(k)) for vl in halves],
            [with_ones(v, vl) for vl in halves],
            shift,
        )
        out_ref[pair, part, :] = out
        lse_ref[pair, part, :] = lse
        return out_of_range(lse)

    def run(shift):
        segments = q_ref.shape[0] // SEG
        if not shift:
            return [segment(slice(i * SEG, (i + 1) * SEG), False) for i in range(segments)]

        @pl.loop(0, segments)
        def _(i):
            segment(pl.ds(pl.multiple_of(i * SEG, SEG), SEG), True)

    with_fallback(run)


def keys_values(tile, half):
    vl = half_mask(tile.shape[0], half)
    zero, one = jnp.zeros_like(tile), jnp.ones_like(tile)
    return jnp.where(vl, zero, tile), jnp.concatenate([jnp.where(vl, tile, zero), one], axis=1)


def near_kernel(count, *refs):
    ins, outs = refs[:4], refs[4:]
    half = lax.rem(lax.axis_index("seq"), 2)
    keys, values = zip(*[keys_values(r[:count, :], half) for r in ins])
    few = count // 2
    vl = half_mask(count, half)

    def run(shift):
        flags = []
        for d in range(4):
            tile = ins[d][count : count + few, :]
            other = swap_halves(tile.astype(f32)).astype(bf16)
            out, lse = attend_one(jnp.concatenate([tile, other], axis=0), keys, values, shift)
            outs[d][...] = encode(out, lse, vl).astype(bf16)
            flags.append(out_of_range(lse))
        return flags

    with_fallback(run)


def far_kernel(base, mid, top, *refs):
    held, gathered, outs = refs[:4], refs[4:8], refs[8:12]
    half = lax.rem(lax.axis_index("seq"), 2)
    blocks = (
        ([r[: 4 * mid, :] for r in gathered], base, mid // 2, 0),
        ([r[4 * mid :, :] for r in gathered], base + mid // 2, top // 2, mid),
    )

    def run(shift):
        flags = []
        for tiles, q_at, few, out_at in blocks:
            keys, values = zip(*[keys_values(t, half) for t in tiles])
            tile = jnp.concatenate([r[q_at : q_at + few, :].astype(f32) for r in held], axis=0)
            q = jnp.concatenate([tile, swap_halves(tile)], axis=0).astype(bf16)
            out, lse = attend_one(q, keys, values, shift)
            found = encode(out, lse, half_mask(8 * few, half))
            for part in range(2):
                for d in range(4):
                    at, start = out_at + part * few, (part * 4 + d) * few
                    outs[d][at : at + few, :] = found[start : start + few, :].astype(bf16)
            flags.append(out_of_range(lse))
        return flags

    with_fallback(run)


def second_kernel(rate, offs_ref, qs, ks, vs, outs_in, lses_in, *refs):
    near, outs, lses = refs[:4], refs[4], refs[5]
    offs = Table(offs_ref)
    count = near[0].shape[0]
    for p in range(2):
        queries, keys, values = [], [], []
        for h in range(2):
            vl = half_mask(count, h)
            picked = pl.ds(offs.of(2 * p + h, 1), count, rate)
            queries.append((qs[p, picked, :] * 0.125).astype(bf16))
            k = ks[p, picked, :]
            keys.append(jnp.where(vl, k, jnp.zeros_like(k)).astype(bf16))
            values.append(with_ones(vs[p, picked, :], vl).astype(bf16))
        out, lse = attend_pair(queries, keys, values, True)
        absorb_pairs(outs, lses, [(p, (offs.of(2 * p, 1), offs.of(2 * p + 1, 1)), out, lse)], rate)
    absorb_coded(outs, lses, [r[...] for r in near], offs, 2, rate, near_place())


def final_kernel(levels, offs_ref, outs_in, lses_in, *refs):
    far, outs, lses, out_any = refs[:4], refs[4], refs[5], refs[6]
    out, sems = refs[7:]
    offs = Table(offs_ref)
    at = 0
    for level, count, rate in levels[1:]:
        coded = [r[at : at + count, :] for r in far]
        absorb_coded(outs, lses, coded, offs, level, rate, far_place())
        at += count
    copies = []
    for i in range(out.shape[0] // SEG):
        part = slice(i * SEG, (i + 1) * SEG)
        for p in range(2):
            out[part, p * LANES : (p + 1) * LANES] = outs[p, part, :].astype(bf16)
        copies.append(pltpu.make_async_copy(out.at[part, :], out_any.at[part, :], sems.at[i]))
        copies[-1].start()
    for copy in copies:
        copy.wait()


def call(
    body, outs, spaces, scratch=(), flops=0, bytes_moved=0, exps=0, aliases=None, out_spaces="", mib=24
):
    whole = pl.BlockSpec(memory_space=VMEM)
    place = {"v": whole, "a": pl.BlockSpec(memory_space=pltpu.HBM), "s": pl.BlockSpec(memory_space=pltpu.SMEM)}
    return pl.pallas_call(
        body,
        out_shape=outs,
        in_specs=[place[c] for c in spaces],
        out_specs=[place[c] for c in out_spaces] if out_spaces else jax.tree.map(lambda _: whole, outs),
        scratch_shapes=list(scratch),
        input_output_aliases=aliases or {},
        compiler_params=pltpu.CompilerParams(vmem_limit_bytes=mib << 20),
        cost_estimate=pl.CostEstimate(flops=flops, bytes_accessed=bytes_moved, transcendentals=exps),
    )


def swapped(shard, bits):
    return lax.ppermute(
        shard, "seq", [(i, i ^ bits) for i in range(lax.axis_size("seq"))]
    )


def per_device(query, key, value, offsets):
    rows, width = query.shape
    places = lax.axis_size("seq")
    rate_three = RATE1 * places // 8
    rate_four = 4 * rate_three
    near_count, mid, top = rows // RATE1, rows // rate_three, rows // rate_four
    levels = (
        (2, near_count, RATE1),
        (3, mid, rate_three),
        (4, top, rate_four),
    )
    offsets = offsets.T
    table = pltpu.SMEM(offsets.shape, jnp.int32)

    def tile(n, kind=bf16):
        return jax.ShapeDtypeStruct((n, LANES), kind)

    wide = jax.ShapeDtypeStruct((2, rows, LANES), f32)
    parts = call(
        lambda *refs: pack_kernel(levels, *refs),
        [tile(near_count * 3 // 2)] * 4
        + [tile((mid + top) * 3 // 2)] * 4
        + [jax.ShapeDtypeStruct(query.shape, bf16)] * 3
        + [wide] * 3,
        "aaaa",
        (table, pltpu.SemaphoreType.DMA((4,))),
        bytes_moved=5 << 20,
        mib=PACK_MIB,
    )(*(pltpu.with_memory_space_constraint(x, pltpu.HBM) for x in (offsets, query, key, value)))
    near_sent, far_sent, narrow, wides = parts[:4], parts[4:8], parts[8:11], parts[11:]
    far_held = [far_sent[0]] + [swapped(far_sent[d], FAR[d]) for d in (1, 2, 3)]
    near_held = [near_sent[0]] + [swapped(near_sent[d], d) for d in (1, 2, 3)]

    state = ()
    for pair in range(2):
        state = call(
            lambda *refs, pair=pair: first_kernel(pair, *refs),
            [wide, wide],
            "vvv" + "v" * len(state),
            flops=2 << 30,
            bytes_moved=4 << 20,
            exps=2 << 20,
            aliases={3: 0, 4: 1} if state else None,
        )(*narrow, *state)

    own_top = jnp.concatenate([r[mid : mid + top] for r in far_held], axis=0)
    other_top = swapped(own_top, 16)
    held = jnp.concatenate([r[:mid] for r in far_held] + [own_top, other_top], axis=0)
    gathered = [held] + [swapped(held, b) for b in (2, 6, 4)]

    near_found = call(
        lambda *refs: near_kernel(near_count, *refs),
        [tile(near_count)] * 4,
        "vvvv",
        flops=6 << 30,
        bytes_moved=2 << 20,
        exps=4 << 20,
    )(*near_held)
    near_back = [near_found[0]] + [swapped(near_found[d], d) for d in (1, 2, 3)]

    far_found = call(
        lambda *refs: far_kernel(mid + top, mid, top, *refs),
        [tile(mid + top)] * 4,
        "v" * 8,
        flops=2 << 30,
        bytes_moved=2 << 20,
        exps=1 << 20,
    )(*far_held, *gathered)
    far_back = [far_found[0]] + [swapped(far_found[d], FAR[d]) for d in (1, 2, 3)]

    state = call(
        lambda *refs: second_kernel(RATE1, *refs),
        [wide, wide],
        "vvvvvvvvvv",
        flops=2 << 30,
        bytes_moved=4 << 20,
        exps=1 << 20,
        aliases={4: 0, 5: 1},
    )(offsets, *wides, *state, *near_back)

    return call(
        lambda *refs: final_kernel(levels, *refs),
        [wide, wide, jax.ShapeDtypeStruct((rows, width), bf16)],
        "vvvvvvv",
        (VMEM((rows, width), bf16), pltpu.SemaphoreType.DMA((rows // SEG,))),
        bytes_moved=6 << 20,
        aliases={1: 0, 2: 1},
        out_spaces="vva",
    )(offsets, *state, *far_back)[2]


def solution(mesh):
    return jax.shard_map(
        per_device,
        mesh=mesh,
        in_specs=(P("seq", "head"), P("seq", "head"), P("seq", "head"), P(None, "head")),
        out_specs=P("seq", "head"),
        check_vma=False,
    )
```
